1024 devices in a mesh: dp: 8 (over y_lo, core), frame: 8 (over x, y_hi), lon: 16 (over z).
Axes of the slice: x: 4, y: 8 (y_hi: 2, y_lo: 4; y = y_hi * 4 + y_lo), z: 16, core: 2. Of those that a mesh axis runs over, the one named last changes fastest.
Arguments:
- fields: bfloat16 [8, 8, 4, 1440, 1024], P('dp', 'frame', None, 'lon'), may hold values from -6 to 6
- band_rows: int32 [8, 4], P('dp'), may hold values from 0 to 719
- earliest_past_snapshot: int32 [8], P('dp'), may hold values from 0 to 7
- lat_table: bfloat16 [720, 1024], replicated, may hold values from -3 to 3
- norm_gain: float32 [1024], replicated, may hold values from 0.5 to 1.5
- w_in1: bfloat16 [2, 16, 64, 64], P(None, 'lon'), may hold values from -0.5 to 0.5
- b_in1: float32 [2, 1024], P(None, 'lon'), may hold values from -1.5 to 1.5
- w_out2: bfloat16 [2, 16, 64, 64], P(None, 'lon'), may hold values from -0.5 to 0.5
- b_out2: float32 [2, 1024], P(None, 'lon'), may hold values from -0.25 to 0.25
- w_query: bfloat16 [1024, 1024], replicated, may hold values from -0.1875 to 0.1875
- w_keyval: bfloat16 [1024, 512], replicated, may hold values from -0.1875 to 0.1875
- w_output: bfloat16 [1024, 1024], replicated, may hold values from -0.1875 to 0.1875
- score_scale: float32 [16], replicated, may hold values from 0.5 to 100
- spec_cot: bfloat16 [8, 8, 4, 2, 368, 1024], P('dp', 'frame', None, None, None, 'lon'), may hold values from -0.01953125 to 0.01953125
Outputs:
- predicted_output_fields: bfloat16 [8, 8, 4, 1440, 1024], P('dp', 'frame', None, 'lon')
- mask_coefficient2_derivative: float32 [2, 16, 64, 64], P(None, 'lon')
- mask_offset2_derivative: float32 [2, 1024], P(None, 'lon')
The draws below stay inside these ranges and needn't reach their ends.
All inputs are finite; a program needn't handle non-finite values.
Results may differ from the reference program's by a relative error of at most 0.03.
Values may be sent and summed in bfloat16 or wider, within the bound.
A program may use at most 64 MiB of HBM per device.

```python
import math
import jax
import jax.numpy as jnp
from jax import lax

D = 1024
LON = 1440
MODES = 368
LAT_ALL = 720
BLK = 64
HD = 64
KVH = 4
LAT_DEV = 4
BATCH = 8
FRAMES = 8
NBLK = 16
HEADS = 16


def draw_band_rows(key, part):
    picked = jax.random.randint(key, (BATCH, LAT_DEV), 0, LAT_ALL, dtype=jnp.int32)
    picked = picked.at[0, 0].set(LAT_ALL - 1)
    return picked.at[0, 1].set(0)


def draw_earliest_past_snapshot(key, part):
    picked = jax.random.randint(key, (BATCH,), 0, FRAMES, dtype=jnp.int32)
    picked = picked.at[0].set(FRAMES - 1)
    return picked.at[1].set(0)


def draw_score_scale(key, part):
    key_base = jax.random.fold_in(key, 0)
    scales = jnp.exp(jax.random.uniform(key_base, (HEADS,), jnp.float32, math.log(0.5), math.log(4.0)))
    return scales.astype(jnp.float32)


def block_levels(stream_key, shape, cuts, low, largest):
    def one(dim, blocks):
        draws = jax.random.uniform(jax.random.fold_in(jax.random.fold_in(stream_key, 6), dim), (blocks,), jnp.float32, low / len(cuts), largest / len(cuts))
        return jnp.repeat(jnp.exp(draws), shape[dim] // blocks).reshape((-1,) + (1,) * (len(shape) - dim - 1))

    level = one(*cuts[0])
    for cut in cuts[1:]:
        level = level * one(*cut)
    return level


def scatter_about(rng, extent, deviation, most, cuts=(), kind=jnp.bfloat16):
    level = block_levels(rng, extent, cuts, -0.22, 0.18) if cuts else 1.0
    result = jax.random.normal(rng, extent, jnp.float32) * deviation * level
    return jnp.minimum(jnp.maximum(result, -most), most).astype(kind)


def setup_inputs(seed: int = 0) -> dict:
    splits = jax.random.split(jax.random.key(seed), 15)
    return {
        "fields": scatter_about(splits[0], (BATCH, FRAMES, LAT_DEV, LON, D), 1.0, 6.0, ((0, 8), (1, 8), (3, 16))),
        "band_rows": draw_band_rows(jax.random.fold_in(splits[14], 71), 0),
        "earliest_past_snapshot": draw_earliest_past_snapshot(jax.random.fold_in(splits[14], 71), 0),
        "lat_table": scatter_about(splits[3], (LAT_ALL, D), 0.5, 3.0),
        "norm_gain": jnp.clip(1.0 + 0.1 * jax.random.normal(splits[4], (D,), jnp.float32), 0.5, 1.5),
        "w_in1": scatter_about(splits[5], (2, NBLK, BLK, BLK), (2 * BLK) ** -0.5, 0.5, ((1, 16),)),
        "b_in1": scatter_about(splits[6], (2, D), 0.3, 1.5, ((1, 16),), jnp.float32),
        "w_out2": scatter_about(splits[7], (2, NBLK, BLK, BLK), (2 * BLK) ** -0.5, 0.5, ((1, 16),)),
        "b_out2": scatter_about(splits[8], (2, D), 0.05, 0.25, ((1, 16),), jnp.float32),
        "w_query": scatter_about(splits[9], (D, D), D ** -0.5, 0.1875),
        "w_keyval": scatter_about(splits[10], (D, 2 * KVH * HD), D ** -0.5, 0.1875),
        "w_output": scatter_about(splits[11], (D, D), D ** -0.5, 0.1875),
        "score_scale": draw_score_scale(jax.random.fold_in(splits[14], 71), 0),
        "spec_cot": scatter_about(splits[13], (BATCH, FRAMES, LAT_DEV, 2, MODES, D), (1.0 / (BATCH * FRAMES * LAT_DEV * MODES) ** 0.5), 0.01953125, ((0, 8), (1, 8), (5, 16))),
    }


def transform_table():
    longitude = jnp.arange(LON, dtype=jnp.int32)
    zonal_wavenumber = jnp.arange(MODES, dtype=jnp.int32)
    turns_mod = longitude[:, None] * zonal_wavenumber[None, :] % LON
    angles = turns_mod.astype(jnp.float32) * (2.0 * math.pi / LON)
    return jnp.concatenate([jnp.cos(angles), -jnp.sin(angles)], axis=1).astype(jnp.bfloat16)

def inverse_table(forward):
    zonal_wavenumber = jnp.arange(MODES, dtype=jnp.int32)
    factor = jnp.where(zonal_wavenumber == 0, 1.0, 2.0).astype(jnp.float32)
    factor = jnp.concatenate([factor, factor])
    return (forward.astype(jnp.float32) * factor[None, :]).astype(jnp.bfloat16)

def block_mix(left, weight):
    return jnp.einsum('rmgc,gce->rmge', left.astype(jnp.float32), weight.astype(jnp.float32))

def filter_modes(spectrum, w_in1, b_in1, w_out2, b_out2):
    spectral_real = spectrum[:, 0]
    spec_im = spectrum[:, 1]
    first_re = jax.nn.relu(block_mix(spectral_real, w_in1[0]) - block_mix(spec_im, w_in1[1]) + b_in1[0]).astype(jnp.bfloat16)
    first_im = jax.nn.relu(block_mix(spectral_real, w_in1[1]) + block_mix(spec_im, w_in1[0]) + b_in1[1]).astype(jnp.bfloat16)
    second_re = (block_mix(first_re, w_out2[0]) - block_mix(first_im, w_out2[1]) + b_out2[0]).astype(jnp.bfloat16)
    second_im = (block_mix(first_re, w_out2[1]) + block_mix(first_im, w_out2[0]) + b_out2[1]).astype(jnp.bfloat16)
    return (first_re, first_im, jnp.concatenate([second_re, second_im], axis=1))

def head_norm(values_in):
    return values_in * lax.rsqrt(lax.optimization_barrier(jnp.mean(values_in * values_in, axis=-1, keepdims=True)) + 1e-06)

def reference(fields, band_rows, earliest_past_snapshot, lat_table, norm_gain, w_in1, b_in1, w_out2, b_out2, w_query, w_keyval, w_output, score_scale, spec_cot):
    forward = transform_table()
    backward = inverse_table(forward)
    scale_t = 1.0 / math.sqrt(LON)
    groups = HEADS // KVH
    onehot = (band_rows[:, :, None] == jnp.arange(LAT_ALL, dtype=jnp.int32)[None, None, :]).astype(jnp.float32)
    embedding = jnp.einsum('blt,td->bld', onehot, lat_table.astype(jnp.float32))
    embed_flat = jnp.broadcast_to(embedding[:, None], (BATCH, FRAMES, LAT_DEV, D)).reshape(BATCH * FRAMES, LAT_DEV, D)
    fields_flat = fields.reshape(BATCH * FRAMES, LAT_DEV, LON, D)
    cot_flat = spec_cot.reshape(BATCH * FRAMES, LAT_DEV, 2, MODES, D)
    offset_first_layer = b_in1.reshape(2, NBLK, BLK)
    bias_two = b_out2.reshape(2, NBLK, BLK)

    def spectral_step(packed):
        snapshot_state, frame_embed, frame_cot = packed
        inputs = snapshot_state.astype(jnp.float32) + frame_embed[:, None, :]
        center = lax.optimization_barrier(jnp.mean(inputs, axis=-1, keepdims=True))
        spread = lax.optimization_barrier(jnp.mean(jnp.square(inputs - center), axis=-1, keepdims=True))
        normed = ((inputs - center) * lax.rsqrt(spread + 1e-05) * norm_gain.astype(jnp.float32)).astype(jnp.bfloat16)
        spectrum = (jnp.einsum('lnd,nk->lkd', normed.astype(jnp.float32), forward.astype(jnp.float32)) * scale_t).astype(jnp.bfloat16)
        spectrum = spectrum.reshape(LAT_DEV, 2, MODES, NBLK, BLK)
        first_re, first_im, mixed = filter_modes(spectrum, w_in1, offset_first_layer, w_out2, bias_two)
        mixed = mixed.reshape(LAT_DEV, 2 * MODES, D)
        grid_part = (jnp.einsum('lkd,nk->lnd', mixed.astype(jnp.float32), backward.astype(jnp.float32)) * scale_t).astype(jnp.bfloat16)
        hidden = (inputs + grid_part.astype(jnp.float32)).astype(jnp.bfloat16)
        cotangent = frame_cot.reshape(LAT_DEV, 2, MODES, NBLK, BLK).astype(jnp.float32)
        real_first = first_re.astype(jnp.float32)
        imag_first = first_im.astype(jnp.float32)
        grad_re = jnp.einsum('lmgc,lmge->gce', real_first, cotangent[:, 0]) + jnp.einsum('lmgc,lmge->gce', imag_first, cotangent[:, 1])
        grad_im = jnp.einsum('lmgc,lmge->gce', real_first, cotangent[:, 1]) - jnp.einsum('lmgc,lmge->gce', imag_first, cotangent[:, 0])
        bias_grad = lax.optimization_barrier(jnp.sum(cotangent, axis=(0, 2))).reshape(2, D)
        return (hidden, jnp.stack([grad_re, grad_im]), bias_grad)
    latent_entire_activation, grad_stack, bias_stack = lax.map(spectral_step, (fields_flat, embed_flat, cot_flat))
    mask_coefficient2_derivative = lax.optimization_barrier(jnp.sum(grad_stack, axis=0))
    mask_offset2_derivative = lax.optimization_barrier(jnp.sum(bias_stack, axis=0))
    latent_entire_activation = latent_entire_activation.reshape(BATCH, FRAMES, LAT_DEV * LON, D)
    site_total = LAT_DEV * LON
    frame_ids = jnp.arange(FRAMES, dtype=jnp.int32)

    def per_example_softmax_mixing(packed):
        hidden_b, first_b = packed
        tokens = hidden_b.reshape(FRAMES * site_total, D)
        query = jnp.dot(tokens, w_query, preferred_element_type=jnp.float32).reshape(FRAMES, site_total, HEADS, HD)
        qnorm = head_norm(query).astype(jnp.bfloat16)
        keyval = jnp.dot(tokens, w_keyval, preferred_element_type=jnp.float32)
        knorm = head_norm(keyval[:, :KVH * HD].reshape(FRAMES, site_total, KVH, HD)).astype(jnp.bfloat16)
        values = keyval[:, KVH * HD:].astype(jnp.bfloat16).reshape(FRAMES, site_total, KVH, HD)
        q_five = qnorm.reshape(FRAMES, site_total, KVH, groups, HD).astype(jnp.float32)
        scores = jnp.einsum('qskgd,tskd->skgqt', q_five, knorm.astype(jnp.float32))
        scores = scores * (score_scale.reshape(KVH, groups, 1, 1) / math.sqrt(HD))
        later = frame_ids[None, :] <= frame_ids[:, None]
        seen = later & ((frame_ids[None, :] >= first_b) | (frame_ids[None, :] == frame_ids[:, None]))
        scores = jnp.where(seen, scores, -1e+30)
        top_score = lax.optimization_barrier(jnp.max(scores, axis=-1, keepdims=True))
        weights = jnp.exp(scores - top_score)
        probs = (weights / lax.optimization_barrier(jnp.sum(weights, axis=-1, keepdims=True))).astype(jnp.bfloat16)
        attended = jnp.einsum('skgqt,tskd->qskgd', probs.astype(jnp.float32), values.astype(jnp.float32)).astype(jnp.bfloat16)
        output = jnp.dot(attended.reshape(FRAMES * site_total, D), w_output, preferred_element_type=jnp.float32)
        return (tokens.astype(jnp.float32) + output).astype(jnp.bfloat16).reshape(FRAMES, LAT_DEV, LON, D)
    predicted_output_fields = lax.map(per_example_softmax_mixing, (latent_entire_activation, earliest_past_snapshot))
    return (predicted_output_fields, mask_coefficient2_derivative, mask_offset2_derivative)
```

```python
import functools
import math

import jax
import jax.numpy as jnp
import numpy as np
from jax import lax
from jax.experimental import pallas as pl
from jax.experimental.pallas import tpu as pltpu
from jax.sharding import PartitionSpec as P

MESH = pl.DeviceIdType.MESH
F32 = jnp.float32
BF16 = jnp.bfloat16


def lanes_below(shape, bound):
    return lax.broadcasted_iota(jnp.int32, shape, len(shape) - 1) < bound


def split_two(value):
    high = value.astype(BF16)
    return high, (value - high.astype(F32)).astype(BF16)


def dot32(left, right, dims=(((1,), (0,)), ((), ()))):
    return lax.dot_general(left, right, dims, preferred_element_type=F32)


def angle_tables(length, local, parts, padded, modes, wide):
    near = np.zeros((2, padded, wide), np.float64)
    far = np.zeros((2, parts, 1, wide), np.float64)
    wave = np.arange(modes)
    turn = 2.0 * np.pi / length
    inner = (np.arange(local)[:, None] * wave[None, :]) % length
    near[0, :local, :modes] = np.cos(turn * inner)
    near[1, :local, :modes] = np.sin(turn * inner)
    outer = (np.arange(parts)[:, None] * local * wave[None, :]) % length
    far[0, :, 0, :modes] = np.cos(turn * outer)
    far[1, :, 0, :modes] = np.sin(turn * outer)
    return near.astype(np.float32), far.astype(np.float32)


def layer_kernel(
    geo,
    first_ref,
    fields_ref,
    embed_ref,
    gain_ref,
    w1_ref,
    b1_ref,
    w2_ref,
    b2_ref,
    near_ref,
    far_ref,
    scale_ref,
    cot_ref,
    wq_hbm,
    wkv_hbm,
    wo_hbm,
    out_ref,
    grad_ref,
    wq,
    wkv,
    wo,
    table,
    mix1,
    mix2,
    brow,
    send1,
    recv1,
    send2,
    recv2,
    sendh,
    recvh,
    sendo,
    recvo,
    qs,
    kx,
    vx,
    scores,
    top,
    total,
    attended,
    acc,
    sums_send,
    sums_recv,
    weight_sem,
    own_sem,
    z_send,
    z_recv,
    f_send,
    f_recv,
    s_send,
    s_recv,
):
    n, nf, nd = geo["lon"], geo["frame"], geo["dp"]
    local, padded, modes, wide = geo["local"], geo["padded"], geo["modes"], geo["wide"]
    width, slab = geo["width"], geo["slab"]
    heads, kv_heads, hd = geo["heads"], geo["kv_heads"], geo["hd"]
    kv_width = kv_heads * hd
    scale_t = 1.0 / math.sqrt(local * n)
    me = lax.axis_index("lon")
    my_frame = lax.axis_index("frame")
    my_dp = lax.axis_index("dp")

    def partner(index, bit):
        return index + bit * (1 - 2 * ((index // bit) % 2))

    sum_steps = []
    bit = 1
    while bit < nd:
        sum_steps.append(("dp", partner(my_dp, bit)))
        bit *= 2
    bit = 1
    while bit < nf:
        sum_steps.append(("frame", partner(my_frame, bit)))
        bit *= 2
    dp_partners = [who for axis, who in sum_steps if axis == "dp"]

    barrier = pltpu.get_barrier_semaphore()

    @pl.loop(1, n)
    def _(o):
        pl.semaphore_signal(
            barrier, inc=1, device_id={"lon": lax.rem(me + o, n)}, device_id_type=MESH
        )

    @pl.loop(1, nf)
    def _(o):
        pl.semaphore_signal(
            barrier, inc=1, device_id={"frame": lax.rem(my_frame + o, nf)}, device_id_type=MESH
        )

    for who in dp_partners:
        pl.semaphore_signal(barrier, inc=1, device_id={"dp": who}, device_id_type=MESH)

    weight_copies = [
        pltpu.make_async_copy(src, dst, weight_sem.at[i])
        for i, (src, dst) in enumerate(((wq_hbm, wq), (wkv_hbm, wkv), (wo_hbm, wo)))
    ]
    for copy in weight_copies:
        copy.start()

    send1[...] = jnp.zeros_like(send1)
    sendh[...] = jnp.zeros_like(sendh)

    def z_copy(src, dst, stage, p, o, target, slot):
        return pltpu.make_async_remote_copy(
            src_ref=src.at[p, target],
            dst_ref=dst.at[p, slot],
            send_sem=z_send.at[stage, p, o],
            recv_sem=z_recv.at[stage, p, o],
            device_id={"lon": target},
            device_id_type=MESH,
        )

    def f_copy(src, dst, stage, p, o, target, slot):
        return pltpu.make_async_remote_copy(
            src_ref=src.at[p, target],
            dst_ref=dst.at[p, slot],
            send_sem=f_send.at[stage, p, o],
            recv_sem=f_recv.at[stage, p, o],
            device_id={"frame": target},
            device_id_type=MESH,
        )

    def start_all(maker, src, dst, stage, p, size, mine, own):
        @pl.loop(1, size)
        def _(o):
            maker(src, dst, stage, p, o, lax.rem(mine + o, size), mine).start()

        pltpu.make_async_copy(src.at[p, mine], dst.at[p, mine], own_sem.at[own, p]).start()

    def wait_recvs(maker, src, dst, stage, p, size, mine, own):
        pltpu.make_async_copy(src.at[p, mine], dst.at[p, mine], own_sem.at[own, p]).wait()

        @pl.loop(1, size)
        def _(o):
            peer = lax.rem(mine + size - o, size)
            maker(src, dst, stage, p, o, peer, peer).wait_recv()

    def wait_sends(maker, src, dst, stage, p, size, mine):
        @pl.loop(1, size)
        def _(o):
            maker(src, dst, stage, p, o, lax.rem(mine + o, size), mine).wait_send()

    half = lanes_below((local, 128), 64)

    def normalize(p, r):
        cells = fields_ref[2 * p + r].astype(F32) + embed_ref[2 * p + r]
        cells = cells - jnp.mean(cells, axis=-1, keepdims=True)
        spread = jnp.mean(cells * cells, axis=-1, keepdims=True)
        return cells * lax.rsqrt(spread + 1e-05) * gain_ref[...]

    @pl.loop(0, 2)
    def _(p):
        row_a = normalize(p, 0)
        row_b = normalize(p, 1)
        for s in range(n // 2):
            part_a = row_a[:, s * 128 : (s + 1) * 128]
            part_b = row_b[:, s * 128 : (s + 1) * 128]
            even = jnp.where(half, part_a, pltpu.roll(part_b, 64, 1))
            odd = jnp.where(half, pltpu.roll(part_a, 64, 1), part_b)
            send1[p, 2 * s, 0:local, :] = even.astype(BF16)
            send1[p, 2 * s + 1, 0:local, :] = odd.astype(BF16)

        @pl.when(p == 0)
        def _():
            pl.semaphore_wait(barrier, (n - 1) + (nf - 1) + len(dp_partners))

        start_all(z_copy, send1, recv1, 0, p, n, me, 0)

    near_cos, near_sin = near_ref[0], near_ref[1]

    @pl.loop(0, n)
    def _(s):
        far_cos, far_sin = far_ref[0, s], far_ref[1, s]
        rows = pl.ds(pl.multiple_of(s * padded, padded), padded)
        table[rows, 0:wide] = (near_cos * far_cos - near_sin * far_sin).astype(BF16)
        table[rows, wide : 2 * wide] = (-(near_sin * far_cos + near_cos * far_sin)).astype(BF16)

    columns = []
    for w_ref, mix, b_ref in ((w1_ref, mix1, b1_ref), (w2_ref, mix2, b2_ref)):
        brow[0:64, 0:64] = w_ref[0].astype(F32)
        brow[0:64, 64:128] = w_ref[1].astype(F32)
        brow[64:128, 0:64] = -w_ref[1].astype(F32)
        brow[64:128, 64:128] = w_ref[0].astype(F32)
        mix[...] = brow[...].T.astype(BF16)
        brow[0:1, 0:64] = b_ref[0:1, :]
        brow[0:1, 64:128] = b_ref[1:2, :]
        columns.append(jnp.broadcast_to(brow[0:1, :], (128, 128)).T[:, 0:1])
    column1, column2 = columns
    wave = lax.broadcasted_iota(jnp.int32, (128, wide), 1)
    factor = jnp.where(wave == 0, 1.0, 2.0)

    acc[...] = jnp.zeros_like(acc)

    @pl.loop(0, 2)
    def _(p):
        wait_recvs(z_copy, send1, recv1, 0, p, n, me, 0)
        gathered = recv1[p].reshape(n * padded, 128)
        spectrum = dot32(gathered.T, table[...]) * scale_t
        cos_part = spectrum[:, 0:wide].astype(BF16)
        sin_part = spectrum[:, wide : 2 * wide].astype(BF16)
        mixed_re, mixed_im = [], []
        for r in range(2):
            stacked = jnp.concatenate(
                [cos_part[64 * r : 64 * r + 64], sin_part[64 * r : 64 * r + 64]], axis=0
            )
            first = jnp.maximum(dot32(mix1[...], stacked) + column1, 0.0).astype(BF16)
            second = (dot32(mix2[...], first) + column2).astype(BF16)
            second = (second.astype(F32) * factor).astype(BF16)
            mixed_re.append(second[0:64])
            mixed_im.append(second[64:128])
            for part in range(2):
                cot = cot_ref[2 * p + r, part]
                acc[part, 0:128, :] += dot32(first[:, 0:modes], cot)
                acc[part, 128:136, :] += jnp.broadcast_to(
                    jnp.sum(cot.astype(F32), axis=0, keepdims=True), (8, 64)
                )
        turned = (((1,), (1,)), ((), ()))
        grid = dot32(table[:, 0:wide], jnp.concatenate(mixed_re, axis=0), turned)
        grid = grid + dot32(table[:, wide : 2 * wide], jnp.concatenate(mixed_im, axis=0), turned)
        send2[p] = (grid * scale_t).astype(BF16).reshape(n, padded, 128)
        start_all(z_copy, send2, recv2, 1, p, n, me, 1)

    sums_send[0, 0:64, :] = acc[0, 0:64, :] + acc[1, 64:128, :]
    sums_send[0, 64:128, :] = acc[1, 0:64, :] - acc[0, 64:128, :]
    sums_send[0, 128:136, :] = acc[0, 128:136, :]
    sums_send[0, 136:144, :] = acc[1, 128:136, :]

    def sum_copy(i):
        axis, who = sum_steps[i]
        return pltpu.make_async_remote_copy(
            src_ref=sums_send.at[i],
            dst_ref=sums_recv.at[i],
            send_sem=s_send.at[i],
            recv_sem=s_recv.at[i],
            device_id={axis: who},
            device_id_type=MESH,
        )

    def finish_sum(i):
        sum_copy(i).wait()
        joined = sums_send[i] + sums_recv[i]
        if i + 1 < len(sum_steps):
            sums_send[i + 1] = joined
            sum_copy(i + 1).start()
        else:
            grad_ref[...] = joined

    early = len(sum_steps) // 2
    sum_copy(0).start()
    for i in range(early):
        finish_sum(i)

    for copy in weight_copies:
        copy.wait()

    lane_head = lax.broadcasted_iota(jnp.int32, (width, 128), 0) // hd
    pool = (lane_head == lax.broadcasted_iota(jnp.int32, (width, 128), 1)).astype(BF16)
    head_lane = lax.broadcasted_iota(jnp.int32, (128, width), 1) // hd
    spread_heads = (head_lane == lax.broadcasted_iota(jnp.int32, (128, width), 0)).astype(BF16)
    rows_all = nf * slab
    half_all = lanes_below((rows_all, 128), 64)
    groups = heads // kv_heads

    def head_norm(value, lanes):
        high, low = split_two(value * value)
        pooled = pool[0:lanes]
        mean = (dot32(high, pooled) + dot32(low, pooled)) * (1.0 / hd)
        high, low = split_two(lax.rsqrt(mean + 1e-06))
        wide_heads = spread_heads[:, 0:lanes]
        return value * (dot32(high, wide_heads) + dot32(low, wide_heads))

    def duplicate(value, ref):
        for j in range(kv_width // 128):
            part = value[:, j * 128 : (j + 1) * 128]
            rolled = pltpu.roll(part, 64, 1)
            ref[:, 2 * j * 128 : (2 * j + 1) * 128] = jnp.where(half_all, part, rolled)
            ref[:, (2 * j + 1) * 128 : (2 * j + 2) * 128] = jnp.where(half_all, rolled, part)

    def per_query_head(ref, t):
        rows = slice(t * slab, (t + 1) * slab)
        parts = []
        for kh in range(kv_heads):
            parts += [ref[rows, kh * 128 : (kh + 1) * 128]] * (groups // 2)
        return jnp.concatenate(parts, axis=1)

    @pl.loop(0, 2)
    def _(p):
        wait_recvs(z_copy, send2, recv2, 1, p, n, me, 1)
        for s in range(n // 2):
            lanes = slice(s * 128, (s + 1) * 128)
            even = recv2[p, 2 * s, 0:local, :].astype(F32)
            odd = recv2[p, 2 * s + 1, 0:local, :].astype(F32)
            grid_rows = (
                jnp.where(half, even, pltpu.roll(odd, 64, 1)),
                jnp.where(half, pltpu.roll(even, 64, 1), odd),
            )
            for r in range(2):
                inputs = fields_ref[2 * p + r, :, lanes].astype(F32) + embed_ref[2 * p + r, :, lanes]
                hidden = (inputs + grid_rows[r]).astype(BF16)
                first_slab = r * padded // slab
                for k in range(padded // slab):
                    count = min(slab, local - k * slab)
                    if count > 0:
                        sendh[p, first_slab + k, 0:count, lanes] = hidden[
                            k * slab : k * slab + count
                        ]
        start_all(f_copy, sendh, recvh, 0, p, nf, my_frame, 2)
        wait_recvs(f_copy, sendh, recvh, 0, p, nf, my_frame, 2)

        tokens = recvh[p].reshape(rows_all, width)
        query = head_norm(dot32(tokens, wq[...]), width)
        qs[...] = query.astype(BF16).astype(F32)
        keyval = dot32(tokens, wkv[...])
        keys = head_norm(keyval[:, 0:kv_width], kv_width)
        duplicate(keys.astype(BF16).astype(F32), kx)
        duplicate(keyval[:, kv_width:].astype(BF16).astype(F32), vx)
        top[...] = jnp.full_like(top, -3e38)
        first_seen = first_ref[0]
        for t in range(nf):
            rows = slice(t * slab, rows_all)
            count = nf - t
            product = (
                qs[rows, :].reshape(count, slab, width) * per_query_head(kx, t)[None]
            ).reshape(count * slab, width)
            high, low = split_two(product)
            score = (dot32(high, pool) + dot32(low, pool)) * scale_ref[...]
            if count > 1:
                later = jnp.where(t >= first_seen, score[slab:], -1e30)
                score = jnp.concatenate([score[0:slab], later], axis=0)
            scores[t, rows, :] = score
            top[rows, :] = jnp.maximum(top[rows, :], score)
        total[...] = jnp.zeros_like(total)
        for t in range(nf):
            rows = slice(t * slab, rows_all)
            weight = jnp.exp(scores[t, rows, :] - top[rows, :])
            scores[t, rows, :] = weight
            total[rows, :] += weight
        attended[...] = jnp.zeros_like(attended)
        for t in range(nf):
            rows = slice(t * slab, rows_all)
            count = nf - t
            probs = (scores[t, rows, :] / total[rows, :]).astype(BF16)
            spread_probs = dot32(probs, spread_heads)
            attended[rows, :] += (
                spread_probs.reshape(count, slab, width) * per_query_head(vx, t)[None]
            ).reshape(count * slab, width)
        output = dot32(attended[...].astype(BF16), wo[...])
        sendo[p] = (tokens.astype(F32) + output).astype(BF16).reshape(nf, slab, width)
        start_all(f_copy, sendo, recvo, 1, p, nf, my_frame, 3)

    for i in range(early, len(sum_steps)):
        finish_sum(i)

    @pl.loop(0, 2)
    def _(p):
        wait_recvs(f_copy, sendo, recvo, 1, p, nf, my_frame, 3)
        for r in range(2):
            first_slab = r * padded // slab
            for k in range(padded // slab):
                count = min(slab, local - k * slab)
                if count > 0:
                    out_ref[2 * p + r, k * slab : k * slab + count, :] = recvo[
                        p, first_slab + k, 0:count, :
                    ]

    @pl.loop(0, 2)
    def _(p):
        wait_sends(z_copy, send1, recv1, 0, p, n, me)
        wait_sends(z_copy, send2, recv2, 1, p, n, me)
        wait_sends(f_copy, sendh, recvh, 0, p, nf, my_frame)
        wait_sends(f_copy, sendo, recvo, 1, p, nf, my_frame)


def body(
    fields,
    band_rows,
    earliest_past_snapshot,
    lat_table,
    norm_gain,
    w_in1,
    b_in1,
    w_out2,
    b_out2,
    w_query,
    w_keyval,
    w_output,
    score_scale,
    spec_cot,
):
    _, _, lat_rows, local, width = fields.shape
    n = lax.axis_size("lon")
    nf = lax.axis_size("frame")
    nd = lax.axis_size("dp")
    modes = spec_cot.shape[4]
    block = w_in1.shape[2]
    heads = score_scale.shape[0]
    hd = width // heads
    kv_heads = w_keyval.shape[1] // 2 // hd
    padded = -(-local // 16) * 16
    wide = -(-modes // 128) * 128
    slab = 2 * padded // nf
    rows_all = 2 * padded
    geo = dict(
        lon=n,
        frame=nf,
        dp=nd,
        local=local,
        padded=padded,
        modes=modes,
        wide=wide,
        width=width,
        slab=slab,
        heads=heads,
        kv_heads=kv_heads,
        hd=hd,
    )
    near, far = angle_tables(local * n, local, n, padded, modes, wide)
    embed = lat_table[band_rows[0]].astype(F32).reshape(lat_rows, 1, width)
    scale_row = jnp.pad(score_scale / math.sqrt(hd), (0, 128 - heads)).reshape(1, 128)
    steps = int(math.log2(nd)) + int(math.log2(nf))
    vmem = pl.BlockSpec(memory_space=pltpu.VMEM)
    smem = pl.BlockSpec(memory_space=pltpu.SMEM)
    anywhere = pl.BlockSpec(memory_space=pl.ANY)
    out, grads = pl.pallas_call(
        functools.partial(layer_kernel, geo),
        out_shape=(
            jax.ShapeDtypeStruct((lat_rows, local, width), BF16),
            jax.ShapeDtypeStruct((144, block), F32),
        ),
        in_specs=[smem] + [vmem] * 11 + [anywhere] * 3,
        out_specs=(vmem, vmem),
        scratch_shapes=[
            pltpu.VMEM(w_query.shape, BF16),
            pltpu.VMEM(w_keyval.shape, BF16),
            pltpu.VMEM(w_output.shape, BF16),
            pltpu.VMEM((n * padded, 2 * wide), BF16),
            pltpu.VMEM((128, 128), BF16),
            pltpu.VMEM((128, 128), BF16),
            pltpu.VMEM((128, 128), F32),
        ]
        + [pltpu.VMEM((2, n, padded, 128), BF16)] * 4
        + [pltpu.VMEM((2, nf, slab, width), BF16)] * 4
        + [
            pltpu.VMEM((rows_all, width), F32),
            pltpu.VMEM((rows_all, kv_heads * 128), F32),
            pltpu.VMEM((rows_all, kv_heads * 128), F32),
            pltpu.VMEM((nf, rows_all, 128), F32),
            pltpu.VMEM((rows_all, 128), F32),
            pltpu.VMEM((rows_all, 128), F32),
            pltpu.VMEM((rows_all, width), F32),
            pltpu.VMEM((2, 136, block), F32),
            pltpu.VMEM((steps, 144, block), F32),
            pltpu.VMEM((steps, 144, block), F32),
            pltpu.SemaphoreType.DMA((3,)),
            pltpu.SemaphoreType.DMA((4, 2)),
            pltpu.SemaphoreType.DMA((2, 2, n)),
            pltpu.SemaphoreType.DMA((2, 2, n)),
            pltpu.SemaphoreType.DMA((2, 2, nf)),
            pltpu.SemaphoreType.DMA((2, 2, nf)),
            pltpu.SemaphoreType.DMA((steps,)),
            pltpu.SemaphoreType.DMA((steps,)),
        ],
        compiler_params=pltpu.CompilerParams(
            collective_id=0, has_side_effects=True, vmem_limit_bytes=60 * 2**20
        ),
        name="layer",
    )(
        earliest_past_snapshot,
        fields.reshape(lat_rows, local, width),
        embed,
        norm_gain.reshape(1, width),
        w_in1.reshape(2, block, block),
        b_in1,
        w_out2.reshape(2, block, block),
        b_out2,
        near,
        far,
        scale_row,
        spec_cot.reshape(lat_rows, 2, modes, block),
        w_query,
        w_keyval,
        w_output,
    )
    return (
        out.reshape(fields.shape),
        grads[0 : 2 * block].reshape(2, 1, block, block),
        jnp.stack([grads[2 * block], grads[2 * block + 8]]),
    )


def solution(mesh):
    placed = (
        P("dp", "frame", None, "lon", None),
        P("dp", None),
        P("dp"),
        P(),
        P(),
        P(None, "lon", None, None),
        P(None, "lon"),
        P(None, "lon", None, None),
        P(None, "lon"),
        P(),
        P(),
        P(),
        P(),
        P("dp", "frame", None, None, None, "lon"),
    )
    return jax.shard_map(
        body,
        mesh=mesh,
        in_specs=placed,
        out_specs=(P("dp", "frame", None, "lon", None), P(None, "lon", None, None), P(None, "lon")),
        check_vma=False,
    )
```

```python
import functools
import math

import jax
import jax.numpy as jnp
import numpy as np
from jax import lax
from jax.experimental import pallas as pl
from jax.experimental.pallas import tpu as pltpu
from jax.sharding import PartitionSpec as P

MESH = pl.DeviceIdType.MESH
EARLY = 3
F32 = jnp.float32
BF16 = jnp.bfloat16


def lanes_below(shape, bound):
    return lax.broadcasted_iota(jnp.int32, shape, len(shape) - 1) < bound


def split_two(value):
    high = value.astype(BF16)
    return high, (value - high.astype(F32)).astype(BF16)


def dot32(left, right, dims=(((1,), (0,)), ((), ()))):
    return lax.dot_general(left, right, dims, preferred_element_type=F32)


def angle_tables(length, local, parts, padded, modes, wide):
    near = np.zeros((2, padded, wide), np.float64)
    far = np.zeros((2, parts, 1, wide), np.float64)
    wave = np.arange(modes)
    turn = 2.0 * np.pi / length
    inner = (np.arange(local)[:, None] * wave[None, :]) % length
    near[0, :local, :modes] = np.cos(turn * inner)
    near[1, :local, :modes] = np.sin(turn * inner)
    outer = (np.arange(parts)[:, None] * local * wave[None, :]) % length
    far[0, :, 0, :modes] = np.cos(turn * outer)
    far[1, :, 0, :modes] = np.sin(turn * outer)
    return near.astype(np.float32), far.astype(np.float32)


def layer_kernel(
    geo,
    first_ref,
    band_ref,
    heads_ref,
    fields_ref,
    lat_ref,
    gain_ref,
    w1_ref,
    b1_ref,
    w2_ref,
    b2_ref,
    near_ref,
    far_ref,
    cot_ref,
    wq_hbm,
    wkv_hbm,
    wo_hbm,
    out_ref,
    grad_ref,
    bias_ref,
    embed,
    wq,
    wkv,
    wo,
    table,
    mix1,
    mix2,
    brow,
    send1,
    recv1,
    send2,
    recv2,
    sendh_a,
    recvh_a,
    sendo_a,
    recvo_a,
    sendh_b,
    recvh_b,
    sendo_b,
    recvo_b,
    qs,
    kx,
    vx,
    scores,
    top,
    total,
    attended,
    acc,
    bias_acc,
    sums_send,
    sums_recv,
    weight_sem,
    own_z_sem,
    own_f_sem,
    z_send,
    z_recv,
    f_send,
    f_recv,
    s_send,
    s_recv,
):
    n, nf, nd = geo["lon"], geo["frame"], geo["dp"]
    local, padded, modes, wide = geo["local"], geo["padded"], geo["modes"], geo["wide"]
    width, pieces = geo["width"], geo["pieces"]
    heads, kv_heads, hd = geo["heads"], geo["kv_heads"], geo["hd"]
    kv_width = kv_heads * hd
    sendh, recvh = (sendh_a, sendh_b), (recvh_a, recvh_b)
    sendo, recvo = (sendo_a, sendo_b), (recvo_a, recvo_b)
    scale_t = 1.0 / math.sqrt(local * n)
    me = lax.axis_index("lon")
    my_frame = lax.axis_index("frame")
    my_dp = lax.axis_index("dp")

    def partner(index, bit):
        return index + bit * (1 - 2 * ((index // bit) % 2))

    sum_steps = []
    bit = 1
    while bit < nd:
        sum_steps.append(("dp", partner(my_dp, bit)))
        bit *= 2
    bit = 1
    while bit < nf:
        sum_steps.append(("frame", partner(my_frame, bit)))
        bit *= 2
    dp_partners = [who for axis, who in sum_steps if axis == "dp"]

    barrier = pltpu.get_barrier_semaphore()

    @pl.loop(1, n)
    def _(o):
        pl.semaphore_signal(
            barrier, inc=1, device_id={"lon": lax.rem(me + o, n)}, device_id_type=MESH
        )

    @pl.loop(1, nf)
    def _(o):
        pl.semaphore_signal(
            barrier, inc=1, device_id={"frame": lax.rem(my_frame + o, nf)}, device_id_type=MESH
        )

    for who in dp_partners:
        pl.semaphore_signal(barrier, inc=1, device_id={"dp": who}, device_id_type=MESH)

    weight_copies = [
        pltpu.make_async_copy(src, dst, weight_sem.at[i])
        for i, (src, dst) in enumerate(((wq_hbm, wq), (wkv_hbm, wkv), (wo_hbm, wo)))
    ]
    for copy in weight_copies:
        copy.start()

    rows_in = lat_ref.shape[0]
    picked = jnp.full((8, rows_in), band_ref[0, 0], jnp.int32)
    sublane = lax.broadcasted_iota(jnp.int32, (8, rows_in), 0)
    for r in range(1, band_ref.shape[1]):
        picked = jnp.where(sublane == r, band_ref[0, r], picked)
    onehot = (lax.broadcasted_iota(jnp.int32, (8, rows_in), 1) == picked).astype(BF16)
    looked_up = dot32(onehot, lat_ref[...])
    for r in range(band_ref.shape[1]):
        embed[r] = looked_up[r : r + 1]

    tail = local // 16 * 16
    send1[:, :, tail:, :] = jnp.zeros((2, n, padded - tail, 128), BF16)
    for piece, (start, span) in enumerate(pieces):
        slab = 2 * span // nf
        for k in range(nf // 2):
            if local - start - k * slab < slab:
                used = max(0, (local - start - k * slab) // 8 * 8)
                for r in range(2):
                    sendh[piece][:, r * nf // 2 + k, used:, :] = jnp.zeros(
                        (2, slab - used, width), BF16
                    )

    peers = n - 1

    def z_offset(i):
        return n // 2 + (i % 2) * ((i + 1) // 2) - (1 - i % 2) * (i // 2)

    def z_copy(src, dst, group, p, rows, i, target, slot):
        return pltpu.make_async_remote_copy(
            src_ref=src.at[p, target, rows],
            dst_ref=dst.at[p, slot, rows],
            send_sem=z_send.at[group, i],
            recv_sem=z_recv.at[group, i],
            device_id={"lon": target},
            device_id_type=MESH,
        )

    def z_own(src, dst, group, p, rows):
        return pltpu.make_async_copy(
            src.at[p, me, rows], dst.at[p, me, rows], own_z_sem.at[group]
        )

    def z_start(src, dst, group, p, rows):
        @pl.loop(0, peers)
        def _(i):
            target = lax.rem(me + z_offset(i), n)
            z_copy(src, dst, group, p, rows, i, target, me).start()

        z_own(src, dst, group, p, rows).start()

    def z_wait(src, dst, group, p, rows):
        z_own(src, dst, group, p, rows).wait()

        @pl.loop(0, peers)
        def _(i):
            peer = lax.rem(me + n - z_offset(i), n)
            z_copy(src, dst, group, p, rows, i, peer, peer).wait_recv()

    def z_sent(src, dst, group, p, rows):
        @pl.loop(0, peers)
        def _(i):
            target = lax.rem(me + z_offset(i), n)
            z_copy(src, dst, group, p, rows, i, target, me).wait_send()

    whole = pl.ds(0, padded)
    chunks = [(p, piece) for p in range(2) for piece in range(len(pieces))]

    def back_args(c):
        p, piece = chunks[c]
        return send2, recv2, 2 + c, p, pl.ds(*pieces[piece])

    def f_copy(src, dst, group, p, o, target, slot):
        return pltpu.make_async_remote_copy(
            src_ref=src.at[p, target],
            dst_ref=dst.at[p, slot],
            send_sem=f_send.at[group, o],
            recv_sem=f_recv.at[group, o],
            device_id={"frame": target},
            device_id_type=MESH,
        )

    def f_own(src, dst, group, p):
        return pltpu.make_async_copy(
            src.at[p, my_frame], dst.at[p, my_frame], own_f_sem.at[group]
        )

    def f_start(src, dst, group, p):
        @pl.loop(1, nf)
        def _(o):
            f_copy(src, dst, group, p, o, lax.rem(my_frame + o, nf), my_frame).start()

        f_own(src, dst, group, p).start()

    def f_wait(src, dst, group, p):
        f_own(src, dst, group, p).wait()

        @pl.loop(1, nf)
        def _(o):
            peer = lax.rem(my_frame + nf - o, nf)
            f_copy(src, dst, group, p, o, peer, peer).wait_recv()

    def f_sent(src, dst, group, p):
        @pl.loop(1, nf)
        def _(o):
            f_copy(src, dst, group, p, o, lax.rem(my_frame + o, nf), my_frame).wait_send()

    def out_args(c):
        p, piece = chunks[c]
        return sendh[piece], recvh[piece], 2 * c, p

    def home_args(c):
        p, piece = chunks[c]
        return sendo[piece], recvo[piece], 2 * c + 1, p

    half = lanes_below((local, 128), 64)

    def normalize(p, r):
        cells = fields_ref[2 * p + r].astype(F32) + embed[2 * p + r]
        cells = cells - jnp.mean(cells, axis=-1, keepdims=True)
        spread = jnp.mean(cells * cells, axis=-1, keepdims=True)
        return cells * lax.rsqrt(spread + 1e-05) * gain_ref[...]

    def fill(p):
        row_a = normalize(p, 0)
        row_b = normalize(p, 1)
        for s in range(n // 2):
            part_a = row_a[:, s * 128 : (s + 1) * 128]
            part_b = row_b[:, s * 128 : (s + 1) * 128]
            even = jnp.where(half, part_a, pltpu.roll(part_b, 64, 1))
            odd = jnp.where(half, pltpu.roll(part_a, 64, 1), part_b)
            send1[p, 2 * s, 0:local, :] = even.astype(BF16)
            send1[p, 2 * s + 1, 0:local, :] = odd.astype(BF16)

    fill(0)
    pl.semaphore_wait(barrier, (n - 1) + (nf - 1) + len(dp_partners))
    z_start(send1, recv1, 0, 0, whole)
    fill(1)
    z_start(send1, recv1, 1, 1, whole)

    near_cos, near_sin = near_ref[0], near_ref[1]

    @pl.loop(0, n)
    def _(s):
        far_cos, far_sin = far_ref[0, s], far_ref[1, s]
        rows = pl.ds(pl.multiple_of(s * padded, padded), padded)
        table[rows, 0:wide] = (near_cos * far_cos - near_sin * far_sin).astype(BF16)
        table[rows, wide : 2 * wide] = (-(near_sin * far_cos + near_cos * far_sin)).astype(BF16)

    columns = []
    for w_ref, mix, b_ref in ((w1_ref, mix1, b1_ref), (w2_ref, mix2, b2_ref)):
        brow[0:64, 0:64] = w_ref[0].astype(F32)
        brow[0:64, 64:128] = w_ref[1].astype(F32)
        brow[64:128, 0:64] = -w_ref[1].astype(F32)
        brow[64:128, 64:128] = w_ref[0].astype(F32)
        mix[...] = brow[...].T.astype(BF16)
        brow[0:1, 0:64] = b_ref[0:1, :]
        brow[0:1, 64:128] = b_ref[1:2, :]
        columns.append(jnp.broadcast_to(brow[0:1, :], (128, 128)).T[:, 0:1])
    column1, column2 = columns
    wave = lax.broadcasted_iota(jnp.int32, (128, wide), 1)
    factor = jnp.where(wave == 0, 1.0, 2.0)

    turned = (((1,), (1,)), ((), ()))
    acc[...] = jnp.zeros_like(acc)
    bias_acc[...] = jnp.zeros_like(bias_acc)

    def transform(p):
        z_wait(send1, recv1, p, p, whole)
        gathered = recv1[p].reshape(n * padded, 128)
        spectrum = dot32(gathered.T, table[...]) * scale_t
        cos_part = spectrum[:, 0:wide].astype(BF16)
        sin_part = spectrum[:, wide : 2 * wide].astype(BF16)
        mixed_re, mixed_im = [], []
        for r in range(2):
            stacked = jnp.concatenate(
                [cos_part[64 * r : 64 * r + 64], sin_part[64 * r : 64 * r + 64]], axis=0
            )
            first = jnp.maximum(dot32(mix1[...], stacked) + column1, 0.0).astype(BF16)
            second = (dot32(mix2[...], first) + column2).astype(BF16)
            second = (second.astype(F32) * factor).astype(BF16)
            mixed_re.append(second[0:64])
            mixed_im.append(second[64:128])
            for part in range(2):
                cot = cot_ref[2 * p + r, part]
                acc[part, 0:128, :] += dot32(first[:, 0:modes], cot, turned)
                bias_acc[part] += jnp.broadcast_to(
                    jnp.sum(cot.astype(F32), axis=1, keepdims=True), (64, 128)
                )
        grid = dot32(table[:, 0:wide], jnp.concatenate(mixed_re, axis=0), turned)
        grid = grid + dot32(table[:, wide : 2 * wide], jnp.concatenate(mixed_im, axis=0), turned)
        send2[p] = (grid * scale_t).astype(BF16).reshape(n, padded, 128)
        for c in range(len(chunks)):
            if chunks[c][0] == p:
                z_start(*back_args(c))

    transform(0)
    transform(1)

    sums_send[0, 0:64, :] = acc[0, 0:64, :] + acc[1, 64:128, :]
    sums_send[0, 64:128, :] = acc[1, 0:64, :] - acc[0, 64:128, :]
    for part in range(2):
        sums_send[0, 128 + 8 * part : 136 + 8 * part, :] = bias_acc[part].T[0:8, :]

    def sum_copy(i):
        axis, who = sum_steps[i]
        return pltpu.make_async_remote_copy(
            src_ref=sums_send.at[i],
            dst_ref=sums_recv.at[i],
            send_sem=s_send.at[i],
            recv_sem=s_recv.at[i],
            device_id={axis: who},
            device_id_type=MESH,
        )

    def finish_sum(i):
        sum_copy(i).wait()
        joined = sums_send[i] + sums_recv[i]
        if i + 1 < len(sum_steps):
            sums_send[i + 1] = joined
            sum_copy(i + 1).start()
        else:
            grad_ref[...] = joined[0:128]
            bias_ref[0:1, :] = joined[128:129]
            bias_ref[1:2, :] = joined[136:137]

    sum_copy(0).start()
    steps = len(sum_steps)
    early = min(EARLY, steps)
    for i in range(early):
        finish_sum(i)

    for copy in weight_copies:
        copy.wait()

    lane_head = lax.broadcasted_iota(jnp.int32, (width, 128), 0) // hd
    pool = (lane_head == lax.broadcasted_iota(jnp.int32, (width, 128), 1)).astype(BF16)
    head_lane = lax.broadcasted_iota(jnp.int32, (128, width), 1) // hd
    spread_heads = (head_lane == lax.broadcasted_iota(jnp.int32, (128, width), 0)).astype(BF16)
    head_ids = lax.broadcasted_iota(jnp.int32, (1, 128), 1)
    score_row = jnp.zeros((1, 128), F32)
    for h in range(heads):
        score_row = jnp.where(head_ids == h, heads_ref[h] * (1.0 / math.sqrt(hd)), score_row)
    groups = heads // kv_heads

    def head_norm(value, lanes):
        high, low = split_two(value * value)
        pooled = pool[0:lanes]
        mean = (dot32(high, pooled) + dot32(low, pooled)) * (1.0 / hd)
        high, low = split_two(lax.rsqrt(mean + 1e-06))
        wide_heads = spread_heads[:, 0:lanes]
        return value * (dot32(high, wide_heads) + dot32(low, wide_heads))

    def duplicate(value, ref):
        rows_all = value.shape[0]
        half_all = lanes_below((rows_all, 128), 64)
        for j in range(kv_width // 128):
            part = value[:, j * 128 : (j + 1) * 128]
            rolled = pltpu.roll(part, 64, 1)
            ref[0:rows_all, 2 * j * 128 : (2 * j + 1) * 128] = jnp.where(half_all, part, rolled)
            ref[0:rows_all, (2 * j + 1) * 128 : (2 * j + 2) * 128] = jnp.where(half_all, rolled, part)

    def per_query_head(ref, t, slab):
        rows = slice(t * slab, (t + 1) * slab)
        parts = []
        for kh in range(kv_heads):
            parts += [ref[rows, kh * 128 : (kh + 1) * 128]] * (groups // 2)
        return jnp.concatenate(parts, axis=1)

    def exchange(c):
        p, piece = chunks[c]
        start, span = pieces[piece]
        slab = 2 * span // nf
        z_wait(*back_args(c))
        count = min(span, local - start)
        near_half = lanes_below((count, 128), 64)
        for s in range(n // 2):
            lanes = slice(s * 128, (s + 1) * 128)
            even = recv2[p, 2 * s, start : start + count, :].astype(F32)
            odd = recv2[p, 2 * s + 1, start : start + count, :].astype(F32)
            grid_rows = (
                jnp.where(near_half, even, pltpu.roll(odd, 64, 1)),
                jnp.where(near_half, pltpu.roll(even, 64, 1), odd),
            )
            for r in range(2):
                inputs = fields_ref[2 * p + r, start : start + count, lanes].astype(F32)
                inputs = inputs + embed[2 * p + r, :, lanes]
                hidden = (inputs + grid_rows[r]).astype(BF16)
                for k in range(nf // 2):
                    used = min(slab, count - k * slab)
                    if used > 0:
                        sendh[piece][p, r * nf // 2 + k, 0:used, lanes] = hidden[
                            k * slab : k * slab + used
                        ]
        f_start(*out_args(c))

    def attend(c):
        p, piece = chunks[c]
        slab = 2 * pieces[piece][1] // nf
        rows_all = nf * slab
        every = slice(0, rows_all)
        f_wait(*out_args(c))
        tokens = recvh[piece][p].reshape(rows_all, width)
        query = head_norm(dot32(tokens, wq[...]), width)
        qs[every, :] = query.astype(BF16).astype(F32)
        keyval = dot32(tokens, wkv[...])
        keys = head_norm(keyval[:, 0:kv_width], kv_width)
        duplicate(keys.astype(BF16).astype(F32), kx)
        duplicate(keyval[:, kv_width:].astype(BF16).astype(F32), vx)
        top[every, :] = jnp.full((rows_all, 128), -3e38, F32)
        first_seen = first_ref[0]
        for t in range(nf):
            rows = slice(t * slab, rows_all)
            count = nf - t
            product = (
                qs[rows, :].reshape(count, slab, width) * per_query_head(kx, t, slab)[None]
            ).reshape(count * slab, width)
            high, low = split_two(product)
            score = (dot32(high, pool) + dot32(low, pool)) * score_row
            if count > 1:
                later = jnp.where(t >= first_seen, score[slab:], -1e30)
                score = jnp.concatenate([score[0:slab], later], axis=0)
            scores[t, rows, :] = score
            top[rows, :] = jnp.maximum(top[rows, :], score)
        total[every, :] = jnp.zeros((rows_all, 128), F32)
        for t in range(nf):
            rows = slice(t * slab, rows_all)
            weight = jnp.exp(scores[t, rows, :] - top[rows, :])
            scores[t, rows, :] = weight
            total[rows, :] += weight
        attended[every, :] = jnp.zeros((rows_all, width), F32)
        for t in range(nf):
            rows = slice(t * slab, rows_all)
            count = nf - t
            probs = (scores[t, rows, :] / total[rows, :]).astype(BF16)
            spread_probs = dot32(probs, spread_heads)
            attended[rows, :] += (
                spread_probs.reshape(count, slab, width) * per_query_head(vx, t, slab)[None]
            ).reshape(count * slab, width)
        output = dot32(attended[every, :].astype(BF16), wo[...])
        sendo[piece][p] = (tokens.astype(F32) + output).astype(BF16).reshape(nf, slab, width)
        f_start(*home_args(c))

    pending = list(range(early, steps))

    def next_sum():
        if pending:
            finish_sum(pending.pop(0))

    last = len(chunks)
    exchange(0)
    next_sum()
    for c in range(1, last):
        exchange(c)
        if c == 1:
            next_sum()
        attend(c - 1)
    attend(last - 1)
    while pending:
        next_sum()

    for c in range(last):
        p, piece = chunks[c]
        start, span = pieces[piece]
        slab = 2 * span // nf
        f_wait(*home_args(c))
        for r in range(2):
            for k in range(nf // 2):
                first = start + k * slab
                used = min(slab, local - first)
                if used > 0:
                    out_ref[2 * p + r, first : first + used, :] = recvo[piece][
                        p, r * nf // 2 + k, 0:used, :
                    ]

    for p in range(2):
        z_sent(send1, recv1, p, p, whole)
    for c in range(last):
        z_sent(*back_args(c))
        f_sent(*out_args(c))
        f_sent(*home_args(c))


def body(
    fields,
    band_rows,
    earliest_past_snapshot,
    lat_table,
    norm_gain,
    w_in1,
    b_in1,
    w_out2,
    b_out2,
    w_query,
    w_keyval,
    w_output,
    score_scale,
    spec_cot,
):
    _, _, lat_rows, local, width = fields.shape
    n = lax.axis_size("lon")
    nf = lax.axis_size("frame")
    nd = lax.axis_size("dp")
    modes = spec_cot.shape[4]
    block = w_in1.shape[2]
    heads = score_scale.shape[0]
    hd = width // heads
    kv_heads = w_keyval.shape[1] // 2 // hd
    padded = -(-local // 16) * 16
    wide = -(-modes // 128) * 128
    units = 2 * padded // nf // 8
    split = (units + 1) // 2 * 4 * nf
    pieces = ((0, split), (split, padded - split))
    rows_all = 2 * split
    geo = dict(
        lon=n,
        frame=nf,
        dp=nd,
        local=local,
        padded=padded,
        modes=modes,
        wide=wide,
        width=width,
        pieces=pieces,
        heads=heads,
        kv_heads=kv_heads,
        hd=hd,
    )
    near, far = angle_tables(local * n, local, n, padded, modes, wide)
    steps = int(math.log2(nd)) + int(math.log2(nf))
    vmem = pl.BlockSpec(memory_space=pltpu.VMEM)
    smem = pl.BlockSpec(memory_space=pltpu.SMEM)
    anywhere = pl.BlockSpec(memory_space=pl.ANY)
    out, grads, bias = pl.pallas_call(
        functools.partial(layer_kernel, geo),
        out_shape=(
            jax.ShapeDtypeStruct((lat_rows, local, width), BF16),
            jax.ShapeDtypeStruct((2 * block, block), F32),
            jax.ShapeDtypeStruct((2, block), F32),
        ),
        in_specs=[smem] * 3 + [vmem] * 10 + [anywhere] * 3,
        out_specs=(vmem, vmem, vmem),
        scratch_shapes=[
            pltpu.VMEM((lat_rows, 1, width), F32),
            pltpu.VMEM(w_query.shape, BF16),
            pltpu.VMEM(w_keyval.shape, BF16),
            pltpu.VMEM(w_output.shape, BF16),
            pltpu.VMEM((n * padded, 2 * wide), BF16),
            pltpu.VMEM((128, 128), BF16),
            pltpu.VMEM((128, 128), BF16),
            pltpu.VMEM((128, 128), F32),
        ]
        + [pltpu.VMEM((2, n, padded, 128), BF16)] * 4
        + [pltpu.VMEM((2, nf, 2 * pieces[0][1] // nf, width), BF16)] * 4
        + [pltpu.VMEM((2, nf, 2 * pieces[1][1] // nf, width), BF16)] * 4
        + [
            pltpu.VMEM((rows_all, width), F32),
            pltpu.VMEM((rows_all, kv_heads * 128), F32),
            pltpu.VMEM((rows_all, kv_heads * 128), F32),
            pltpu.VMEM((nf, rows_all, 128), F32),
            pltpu.VMEM((rows_all, 128), F32),
            pltpu.VMEM((rows_all, 128), F32),
            pltpu.VMEM((rows_all, width), F32),
            pltpu.VMEM((2, 128, block), F32),
            pltpu.VMEM((2, block, 128), F32),
            pltpu.VMEM((steps, 144, block), F32),
            pltpu.VMEM((steps, 144, block), F32),
            pltpu.SemaphoreType.DMA((3,)),
            pltpu.SemaphoreType.DMA((6,)),
            pltpu.SemaphoreType.DMA((8,)),
            pltpu.SemaphoreType.DMA((6, n - 1)),
            pltpu.SemaphoreType.DMA((6, n - 1)),
            pltpu.SemaphoreType.DMA((8, nf)),
            pltpu.SemaphoreType.DMA((8, nf)),
            pltpu.SemaphoreType.DMA((steps,)),
            pltpu.SemaphoreType.DMA((steps,)),
        ],
        compiler_params=pltpu.CompilerParams(
            collective_id=0, has_side_effects=True, vmem_limit_bytes=60 * 2**20
        ),
        name="layer",
    )(
        earliest_past_snapshot,
        band_rows,
        score_scale,
        fields.reshape(lat_rows, local, width),
        lat_table,
        norm_gain.reshape(1, width),
        w_in1.reshape(2, block, block),
        b_in1,
        w_out2.reshape(2, block, block),
        b_out2,
        near,
        far,
        spec_cot.reshape(lat_rows, 2, modes, block).transpose(0, 1, 3, 2),
        w_query,
        w_keyval,
        w_output,
    )
    return (
        out.reshape(fields.shape),
        grads.reshape(2, 1, block, block),
        bias,
    )


def solution(mesh):
    placed = (
        P("dp", "frame", None, "lon", None),
        P("dp", None),
        P("dp"),
        P(),
        P(),
        P(None, "lon", None, None),
        P(None, "lon"),
        P(None, "lon", None, None),
        P(None, "lon"),
        P(),
        P(),
        P(),
        P(),
        P("dp", "frame", None, None, None, "lon"),
    )
    return jax.shard_map(
        body,
        mesh=mesh,
        in_specs=placed,
        out_specs=(P("dp", "frame", None, "lon", None), P(None, "lon", None, None), P(None, "lon")),
        check_vma=False,
    )
```

```python
import functools
import math

import jax
import jax.numpy as jnp
import numpy as np
from jax import lax
from jax.experimental import pallas as pl
from jax.experimental.pallas import tpu as pltpu
from jax.sharding import PartitionSpec as P

MESH = pl.DeviceIdType.MESH
EARLY = 3
F32 = jnp.float32
BF16 = jnp.bfloat16


def lanes_below(shape, bound):
    return lax.broadcasted_iota(jnp.int32, shape, len(shape) - 1) < bound


def split_two(value):
    high = value.astype(BF16)
    return high, (value - high.astype(F32)).astype(BF16)


def dot32(left, right, dims=(((1,), (0,)), ((), ()))):
    return lax.dot_general(left, right, dims, preferred_element_type=F32)


def angle_tables(length, local, parts, padded, modes, wide):
    near = np.zeros((2, padded, wide), np.float64)
    far = np.zeros((2, parts, 1, wide), np.float64)
    wave = np.arange(modes)
    turn = 2.0 * np.pi / length
    inner = (np.arange(local)[:, None] * wave[None, :]) % length
    near[0, :local, :modes] = np.cos(turn * inner)
    near[1, :local, :modes] = np.sin(turn * inner)
    outer = (np.arange(parts)[:, None] * local * wave[None, :]) % length
    far[0, :, 0, :modes] = np.cos(turn * outer)
    far[1, :, 0, :modes] = np.sin(turn * outer)
    return near.astype(np.float32), far.astype(np.float32)


def layer_kernel(
    geo,
    first_ref,
    band_ref,
    heads_ref,
    fields_ref,
    lat_ref,
    gain_ref,
    w1_ref,
    b1_ref,
    w2_ref,
    b2_ref,
    near_ref,
    far_ref,
    cot_ref,
    wq_hbm,
    wkv_hbm,
    wo_hbm,
    out_ref,
    grad_ref,
    bias_ref,
    embed,
    wq,
    wkv,
    wo,
    table,
    mix1,
    mix2,
    brow,
    send1,
    recv1,
    send2,
    recv2,
    sendh_a,
    recvh_a,
    sendo_a,
    recvo_a,
    sendh_b,
    recvh_b,
    sendo_b,
    recvo_b,
    sendkv,
    recvkv,
    qs,
    kx,
    vx,
    scores,
    top,
    total,
    attended,
    acc,
    bias_acc,
    sums_send,
    sums_recv,
    weight_sem,
    own_z_sem,
    own_f_sem,
    kv_send,
    kv_recv,
    z_send,
    z_recv,
    f_send,
    f_recv,
    s_send,
    s_recv,
):
    n, nf, nd = geo["lon"], geo["frame"], geo["dp"]
    local, padded, modes, wide = geo["local"], geo["padded"], geo["modes"], geo["wide"]
    width, pieces = geo["width"], geo["pieces"]
    heads, kv_heads, hd = geo["heads"], geo["kv_heads"], geo["hd"]
    kv_width = kv_heads * hd
    sendh, recvh = (sendh_a, sendh_b), (recvh_a, recvh_b)
    sendo, recvo = (sendo_a, sendo_b), (recvo_a, recvo_b)
    scale_t = 1.0 / math.sqrt(local * n)
    me = lax.axis_index("lon")
    my_frame = lax.axis_index("frame")
    my_dp = lax.axis_index("dp")
    nx = nf // 2
    my_x, side = my_frame // 2, lax.rem(my_frame, 2)
    other_side = my_x * 2 + 1 - side

    def partner(index, bit):
        return index + bit * (1 - 2 * ((index // bit) % 2))

    sum_steps = []
    bit = 1
    while bit < nd:
        sum_steps.append(("dp", partner(my_dp, bit)))
        bit *= 2
    bit = 1
    while bit < nf:
        sum_steps.append(("frame", partner(my_frame, bit)))
        bit *= 2
    dp_partners = [who for axis, who in sum_steps if axis == "dp"]

    barrier = pltpu.get_barrier_semaphore()

    @pl.loop(1, n)
    def _(o):
        pl.semaphore_signal(
            barrier, inc=1, device_id={"lon": lax.rem(me + o, n)}, device_id_type=MESH
        )

    @pl.loop(1, nx)
    def _(o):
        pl.semaphore_signal(
            barrier,
            inc=1,
            device_id={"frame": lax.rem(my_x + o, nx) * 2 + side},
            device_id_type=MESH,
        )

    pl.semaphore_signal(barrier, inc=1, device_id={"frame": other_side}, device_id_type=MESH)

    for who in dp_partners:
        pl.semaphore_signal(barrier, inc=1, device_id={"dp": who}, device_id_type=MESH)

    weight_copies = [
        pltpu.make_async_copy(src, dst, weight_sem.at[i])
        for i, (src, dst) in enumerate(((wq_hbm, wq), (wkv_hbm, wkv), (wo_hbm, wo)))
    ]
    for copy in weight_copies:
        copy.start()

    rows_in = lat_ref.shape[0]
    picked = jnp.full((8, rows_in), band_ref[0, 0], jnp.int32)
    sublane = lax.broadcasted_iota(jnp.int32, (8, rows_in), 0)
    for r in range(1, band_ref.shape[1]):
        picked = jnp.where(sublane == r, band_ref[0, r], picked)
    onehot = (lax.broadcasted_iota(jnp.int32, (8, rows_in), 1) == picked).astype(BF16)
    looked_up = dot32(onehot, lat_ref[...])
    for r in range(band_ref.shape[1]):
        embed[r] = looked_up[r : r + 1]

    tail = local // 16 * 16
    send1[:, :, tail:, :] = jnp.zeros((2, n, padded - tail, 128), BF16)
    for piece, (start, span) in enumerate(pieces):
        slab = 2 * span // nx
        for k in range(nx // 2):
            if local - start - k * slab < slab:
                used = max(0, (local - start - k * slab) // 8 * 8)
                for r in range(2):
                    sendh[piece][:, r * nx // 2 + k, used:, :] = jnp.zeros(
                        (2, slab - used, width), BF16
                    )

    peers = n - 1

    def z_offset(i):
        return n // 2 + (i % 2) * ((i + 1) // 2) - (1 - i % 2) * (i // 2)

    def z_copy(src, dst, group, p, rows, i, target, slot):
        return pltpu.make_async_remote_copy(
            src_ref=src.at[p, target, rows],
            dst_ref=dst.at[p, slot, rows],
            send_sem=z_send.at[group, i],
            recv_sem=z_recv.at[group, i],
            device_id={"lon": target},
            device_id_type=MESH,
        )

    def z_own(src, dst, group, p, rows):
        return pltpu.make_async_copy(
            src.at[p, me, rows], dst.at[p, me, rows], own_z_sem.at[group]
        )

    def z_start(src, dst, group, p, rows):
        @pl.loop(0, peers)
        def _(i):
            target = lax.rem(me + z_offset(i), n)
            z_copy(src, dst, group, p, rows, i, target, me).start()

        z_own(src, dst, group, p, rows).start()

    def z_wait(src, dst, group, p, rows):
        z_own(src, dst, group, p, rows).wait()

        @pl.loop(0, peers)
        def _(i):
            peer = lax.rem(me + n - z_offset(i), n)
            z_copy(src, dst, group, p, rows, i, peer, peer).wait_recv()

    def z_sent(src, dst, group, p, rows):
        @pl.loop(0, peers)
        def _(i):
            target = lax.rem(me + z_offset(i), n)
            z_copy(src, dst, group, p, rows, i, target, me).wait_send()

    whole = pl.ds(0, padded)
    chunks = [(p, piece) for p in range(2) for piece in range(len(pieces))]

    def back_args(c):
        p, piece = chunks[c]
        return send2, recv2, 2 + c, p, pl.ds(*pieces[piece])

    def f_copy(src, dst, group, p, o, target, slot):
        return pltpu.make_async_remote_copy(
            src_ref=src.at[p, target],
            dst_ref=dst.at[p, slot],
            send_sem=f_send.at[group, o],
            recv_sem=f_recv.at[group, o],
            device_id={"frame": target * 2 + side},
            device_id_type=MESH,
        )

    def f_own(src, dst, group, p):
        return pltpu.make_async_copy(src.at[p, my_x], dst.at[p, my_x], own_f_sem.at[group])

    def f_start(src, dst, group, p):
        @pl.loop(1, nx)
        def _(o):
            f_copy(src, dst, group, p, o, lax.rem(my_x + o, nx), my_x).start()

        f_own(src, dst, group, p).start()

    def f_wait(src, dst, group, p):
        f_own(src, dst, group, p).wait()

        @pl.loop(1, nx)
        def _(o):
            peer = lax.rem(my_x + nx - o, nx)
            f_copy(src, dst, group, p, o, peer, peer).wait_recv()

    def f_sent(src, dst, group, p):
        @pl.loop(1, nx)
        def _(o):
            f_copy(src, dst, group, p, o, lax.rem(my_x + o, nx), my_x).wait_send()

    def kv_copy(c):
        rows = pl.ds(0, 2 * pieces[chunks[c][1]][1])
        return pltpu.make_async_remote_copy(
            src_ref=sendkv.at[c, rows],
            dst_ref=recvkv.at[c, rows],
            send_sem=kv_send.at[c],
            recv_sem=kv_recv.at[c],
            device_id={"frame": other_side},
            device_id_type=MESH,
        )

    def out_args(c):
        p, piece = chunks[c]
        return sendh[piece], recvh[piece], 2 * c, p

    def home_args(c):
        p, piece = chunks[c]
        return sendo[piece], recvo[piece], 2 * c + 1, p

    half = lanes_below((local, 128), 64)

    def normalize(p, r):
        cells = fields_ref[2 * p + r].astype(F32) + embed[2 * p + r]
        cells = cells - jnp.mean(cells, axis=-1, keepdims=True)
        spread = jnp.mean(cells * cells, axis=-1, keepdims=True)
        return cells * lax.rsqrt(spread + 1e-05) * gain_ref[...]

    def fill(p):
        row_a = normalize(p, 0)
        row_b = normalize(p, 1)
        for s in range(n // 2):
            part_a = row_a[:, s * 128 : (s + 1) * 128]
            part_b = row_b[:, s * 128 : (s + 1) * 128]
            even = jnp.where(half, part_a, pltpu.roll(part_b, 64, 1))
            odd = jnp.where(half, pltpu.roll(part_a, 64, 1), part_b)
            send1[p, 2 * s, 0:local, :] = even.astype(BF16)
            send1[p, 2 * s + 1, 0:local, :] = odd.astype(BF16)

    fill(0)
    pl.semaphore_wait(barrier, (n - 1) + nx + len(dp_partners))
    z_start(send1, recv1, 0, 0, whole)
    fill(1)
    z_start(send1, recv1, 1, 1, whole)

    near_cos, near_sin = near_ref[0], near_ref[1]

    @pl.loop(0, n)
    def _(s):
        far_cos, far_sin = far_ref[0, s], far_ref[1, s]
        rows = pl.ds(pl.multiple_of(s * padded, padded), padded)
        table[rows, 0:wide] = (near_cos * far_cos - near_sin * far_sin).astype(BF16)
        table[rows, wide : 2 * wide] = (-(near_sin * far_cos + near_cos * far_sin)).astype(BF16)

    columns = []
    for w_ref, mix, b_ref in ((w1_ref, mix1, b1_ref), (w2_ref, mix2, b2_ref)):
        brow[0:64, 0:64] = w_ref[0].astype(F32)
        brow[0:64, 64:128] = w_ref[1].astype(F32)
        brow[64:128, 0:64] = -w_ref[1].astype(F32)
        brow[64:128, 64:128] = w_ref[0].astype(F32)
        mix[...] = brow[...].T.astype(BF16)
        brow[0:1, 0:64] = b_ref[0:1, :]
        brow[0:1, 64:128] = b_ref[1:2, :]
        columns.append(jnp.broadcast_to(brow[0:1, :], (128, 128)).T[:, 0:1])
    column1, column2 = columns
    wave = lax.broadcasted_iota(jnp.int32, (128, wide), 1)
    factor = jnp.where(wave == 0, 1.0, 2.0)

    turned = (((1,), (1,)), ((), ()))
    acc[...] = jnp.zeros_like(acc)
    bias_acc[...] = jnp.zeros_like(bias_acc)

    def transform(p):
        z_wait(send1, recv1, p, p, whole)
        gathered = recv1[p].reshape(n * padded, 128)
        spectrum = dot32(gathered.T, table[...]) * scale_t
        cos_part = spectrum[:, 0:wide].astype(BF16)
        sin_part = spectrum[:, wide : 2 * wide].astype(BF16)
        mixed_re, mixed_im = [], []
        for r in range(2):
            stacked = jnp.concatenate(
                [cos_part[64 * r : 64 * r + 64], sin_part[64 * r : 64 * r + 64]], axis=0
            )
            first = jnp.maximum(dot32(mix1[...], stacked) + column1, 0.0).astype(BF16)
            second = (dot32(mix2[...], first) + column2).astype(BF16)
            second = (second.astype(F32) * factor).astype(BF16)
            mixed_re.append(second[0:64])
            mixed_im.append(second[64:128])
            for part in range(2):
                cot = cot_ref[2 * p + r, part]
                acc[part, 0:128, :] += dot32(first[:, 0:modes], cot, turned)
                bias_acc[part] += jnp.broadcast_to(
                    jnp.sum(cot.astype(F32), axis=1, keepdims=True), (64, 128)
                )
        grid = dot32(table[:, 0:wide], jnp.concatenate(mixed_re, axis=0), turned)
        grid = grid + dot32(table[:, wide : 2 * wide], jnp.concatenate(mixed_im, axis=0), turned)
        send2[p] = (grid * scale_t).astype(BF16).reshape(n, padded, 128)
        for c in range(len(chunks)):
            if chunks[c][0] == p:
                z_start(*back_args(c))

    transform(0)
    transform(1)

    sums_send[0, 0:64, :] = acc[0, 0:64, :] + acc[1, 64:128, :]
    sums_send[0, 64:128, :] = acc[1, 0:64, :] - acc[0, 64:128, :]
    for part in range(2):
        sums_send[0, 128 + 8 * part : 136 + 8 * part, :] = bias_acc[part].T[0:8, :]

    def sum_copy(i):
        axis, who = sum_steps[i]
        return pltpu.make_async_remote_copy(
            src_ref=sums_send.at[i],
            dst_ref=sums_recv.at[i],
            send_sem=s_send.at[i],
            recv_sem=s_recv.at[i],
            device_id={axis: who},
            device_id_type=MESH,
        )

    def finish_sum(i):
        sum_copy(i).wait()
        joined = sums_send[i] + sums_recv[i]
        if i + 1 < len(sum_steps):
            sums_send[i + 1] = joined
            sum_copy(i + 1).start()
        else:
            grad_ref[...] = joined[0:128]
            bias_ref[0:1, :] = joined[128:129]
            bias_ref[1:2, :] = joined[136:137]

    sum_copy(0).start()
    steps = len(sum_steps)
    early = min(EARLY, steps)
    for i in range(early):
        finish_sum(i)

    for copy in weight_copies:
        copy.wait()

    lane_head = lax.broadcasted_iota(jnp.int32, (width, 128), 0) // hd
    pool = (lane_head == lax.broadcasted_iota(jnp.int32, (width, 128), 1)).astype(BF16)
    head_lane = lax.broadcasted_iota(jnp.int32, (128, width), 1) // hd
    spread_heads = (head_lane == lax.broadcasted_iota(jnp.int32, (128, width), 0)).astype(BF16)
    head_ids = lax.broadcasted_iota(jnp.int32, (1, 128), 1)
    score_row = jnp.zeros((1, 128), F32)
    for h in range(heads):
        score_row = jnp.where(head_ids == h, heads_ref[h] * (1.0 / math.sqrt(hd)), score_row)
    groups = heads // kv_heads

    def head_norm(value, lanes):
        high, low = split_two(value * value)
        pooled = pool[0:lanes]
        mean = (dot32(high, pooled) + dot32(low, pooled)) * (1.0 / hd)
        high, low = split_two(lax.rsqrt(mean + 1e-06))
        wide_heads = spread_heads[:, 0:lanes]
        return value * (dot32(high, wide_heads) + dot32(low, wide_heads))

    def duplicate(value, ref, slot, half_id):
        rows_all = value.shape[0]
        half_all = lanes_below((rows_all, 128), 64)
        for j in range(kv_width // 128):
            part = value[:, j * 128 : (j + 1) * 128]
            rolled = pltpu.roll(part, 64, 1)
            low, high = slice(2 * j * 128, (2 * j + 1) * 128), slice(
                (2 * j + 1) * 128, (2 * j + 2) * 128
            )
            ref[slot, half_id, 0:rows_all, low] = jnp.where(half_all, part, rolled)
            ref[slot, half_id, 0:rows_all, high] = jnp.where(half_all, rolled, part)

    def per_query_head(ref, slot, half_id, t, slab):
        rows = slice(t * slab, (t + 1) * slab)
        parts = []
        for kh in range(kv_heads):
            parts += [ref[slot, half_id, rows, kh * 128 : (kh + 1) * 128]] * (groups // 2)
        return jnp.concatenate(parts, axis=1)

    def exchange(c):
        p, piece = chunks[c]
        start, span = pieces[piece]
        slab = 2 * span // nx
        z_wait(*back_args(c))
        count = min(span, local - start)
        near_half = lanes_below((count, 128), 64)
        for s in range(n // 2):
            lanes = slice(s * 128, (s + 1) * 128)
            even = recv2[p, 2 * s, start : start + count, :].astype(F32)
            odd = recv2[p, 2 * s + 1, start : start + count, :].astype(F32)
            grid_rows = (
                jnp.where(near_half, even, pltpu.roll(odd, 64, 1)),
                jnp.where(near_half, pltpu.roll(even, 64, 1), odd),
            )
            for r in range(2):
                inputs = fields_ref[2 * p + r, start : start + count, lanes].astype(F32)
                inputs = inputs + embed[2 * p + r, :, lanes]
                hidden = (inputs + grid_rows[r]).astype(BF16)
                for k in range(nx // 2):
                    used = min(slab, count - k * slab)
                    if used > 0:
                        sendh[piece][p, r * nx // 2 + k, 0:used, lanes] = hidden[
                            k * slab : k * slab + used
                        ]
        f_start(*out_args(c))

    first_seen = first_ref[0]

    def project(c):
        p, piece = chunks[c]
        rows_all = 2 * pieces[piece][1]
        every = slice(0, rows_all)
        slot = c % 2
        f_wait(*out_args(c))
        tokens = recvh[piece][p].reshape(rows_all, width)
        keyval = dot32(tokens, wkv[...])
        keys = head_norm(keyval[:, 0:kv_width], kv_width).astype(BF16)
        values = keyval[:, kv_width:].astype(BF16)
        sendkv[c, every, 0:kv_width] = keys
        sendkv[c, every, kv_width : 2 * kv_width] = values
        kv_copy(c).start()
        query = head_norm(dot32(tokens, wq[...]), width)
        qs[slot, every, :] = query.astype(BF16).astype(F32)
        duplicate(keys.astype(F32), kx, slot, 0)
        duplicate(values.astype(F32), vx, slot, 0)

    def score_half(c, half_id):
        slab = 2 * pieces[chunks[c][1]][1] // nx
        slot = c % 2
        for j in range(nx):
            rows = slice(j * slab, nx * slab)
            count = nx - j
            product = (
                qs[slot, rows, :].reshape(count, slab, width)
                * per_query_head(kx, slot, half_id, j, slab)[None]
            ).reshape(count * slab, width)
            high, low = split_two(product)
            score = (dot32(high, pool) + dot32(low, pool)) * score_row
            frame = 2 * j + (side if half_id == 0 else 1 - side)
            seen = frame >= first_seen
            same = score[0:slab]
            if half_id == 1:
                same = jnp.where(jnp.logical_and(seen, side == 1), same, -1e30)
            if count > 1:
                later = jnp.where(seen, score[slab:], -1e30)
                score = jnp.concatenate([same, later], axis=0)
            else:
                score = same
            scores[half_id * nx + j, rows, :] = score
            top[rows, :] = jnp.maximum(top[rows, :], score)

    def attend(c):
        p, piece = chunks[c]
        rows_all = 2 * pieces[piece][1]
        slab = rows_all // nx
        every = slice(0, rows_all)
        slot = c % 2
        top[every, :] = jnp.full((rows_all, 128), -3e38, F32)
        score_half(c, 0)
        kv_copy(c).wait_recv()
        keyval = recvkv[c, every, :].astype(F32)
        duplicate(keyval[:, 0:kv_width], kx, slot, 1)
        duplicate(keyval[:, kv_width:], vx, slot, 1)
        score_half(c, 1)
        total[every, :] = jnp.zeros((rows_all, 128), F32)
        for t in range(2 * nx):
            rows = slice(t % nx * slab, rows_all)
            weight = jnp.exp(scores[t, rows, :] - top[rows, :])
            scores[t, rows, :] = weight
            total[rows, :] += weight
        attended[every, :] = jnp.zeros((rows_all, width), F32)
        for t in range(2 * nx):
            j = t % nx
            rows = slice(j * slab, rows_all)
            count = nx - j
            probs = (scores[t, rows, :] / total[rows, :]).astype(BF16)
            spread_probs = dot32(probs, spread_heads)
            attended[rows, :] += (
                spread_probs.reshape(count, slab, width)
                * per_query_head(vx, slot, t // nx, j, slab)[None]
            ).reshape(count * slab, width)
        tokens = recvh[piece][p].reshape(rows_all, width)
        output = dot32(attended[every, :].astype(BF16), wo[...])
        sendo[piece][p] = (tokens.astype(F32) + output).astype(BF16).reshape(nx, slab, width)
        f_start(*home_args(c))

    pending = list(range(early, steps))

    def next_sum():
        if pending:
            finish_sum(pending.pop(0))

    last = len(chunks)
    exchange(0)
    next_sum()
    project(0)
    exchange(1)
    next_sum()
    project(1)
    attend(0)
    exchange(2)
    attend(1)
    project(2)
    exchange(3)
    project(3)
    attend(2)
    attend(3)
    while pending:
        next_sum()

    for c in range(last):
        p, piece = chunks[c]
        start, span = pieces[piece]
        slab = 2 * span // nx
        f_wait(*home_args(c))
        for r in range(2):
            for k in range(nx // 2):
                first = start + k * slab
                used = min(slab, local - first)
                if used > 0:
                    out_ref[2 * p + r, first : first + used, :] = recvo[piece][
                        p, r * nx // 2 + k, 0:used, :
                    ]

    for p in range(2):
        z_sent(send1, recv1, p, p, whole)
    for c in range(last):
        z_sent(*back_args(c))
        f_sent(*out_args(c))
        f_sent(*home_args(c))
        kv_copy(c).wait_send()


def body(
    fields,
    band_rows,
    earliest_past_snapshot,
    lat_table,
    norm_gain,
    w_in1,
    b_in1,
    w_out2,
    b_out2,
    w_query,
    w_keyval,
    w_output,
    score_scale,
    spec_cot,
):
    _, _, lat_rows, local, width = fields.shape
    n = lax.axis_size("lon")
    nf = lax.axis_size("frame")
    nd = lax.axis_size("dp")
    modes = spec_cot.shape[4]
    block = w_in1.shape[2]
    heads = score_scale.shape[0]
    hd = width // heads
    kv_heads = w_keyval.shape[1] // 2 // hd
    padded = -(-local // 16) * 16
    wide = -(-modes // 128) * 128
    nx = nf // 2
    units = 2 * padded // nx // 16
    split = (units + 1) // 2 * 8 * nx
    pieces = ((0, split), (split, padded - split))
    rows_all = 2 * split
    geo = dict(
        lon=n,
        frame=nf,
        dp=nd,
        local=local,
        padded=padded,
        modes=modes,
        wide=wide,
        width=width,
        pieces=pieces,
        heads=heads,
        kv_heads=kv_heads,
        hd=hd,
    )
    near, far = angle_tables(local * n, local, n, padded, modes, wide)
    steps = int(math.log2(nd)) + int(math.log2(nf))
    vmem = pl.BlockSpec(memory_space=pltpu.VMEM)
    smem = pl.BlockSpec(memory_space=pltpu.SMEM)
    anywhere = pl.BlockSpec(memory_space=pl.ANY)
    out, grads, bias = pl.pallas_call(
        functools.partial(layer_kernel, geo),
        out_shape=(
            jax.ShapeDtypeStruct((lat_rows, local, width), BF16),
            jax.ShapeDtypeStruct((2 * block, block), F32),
            jax.ShapeDtypeStruct((2, block), F32),
        ),
        in_specs=[smem] * 3 + [vmem] * 10 + [anywhere] * 3,
        out_specs=(vmem, vmem, vmem),
        scratch_shapes=[
            pltpu.VMEM((lat_rows, 1, width), F32),
            pltpu.VMEM(w_query.shape, BF16),
            pltpu.VMEM(w_keyval.shape, BF16),
            pltpu.VMEM(w_output.shape, BF16),
            pltpu.VMEM((n * padded, 2 * wide), BF16),
            pltpu.VMEM((128, 128), BF16),
            pltpu.VMEM((128, 128), BF16),
            pltpu.VMEM((128, 128), F32),
        ]
        + [pltpu.VMEM((2, n, padded, 128), BF16)] * 4
        + [pltpu.VMEM((2, nx, 2 * pieces[0][1] // nx, width), BF16)] * 4
        + [pltpu.VMEM((2, nx, 2 * pieces[1][1] // nx, width), BF16)] * 4
        + [
            pltpu.VMEM((4, rows_all, w_keyval.shape[1]), BF16),
            pltpu.VMEM((4, rows_all, w_keyval.shape[1]), BF16),
            pltpu.VMEM((2, rows_all, width), F32),
            pltpu.VMEM((2, 2, rows_all, kv_heads * 128), F32),
            pltpu.VMEM((2, 2, rows_all, kv_heads * 128), F32),
            pltpu.VMEM((nf, rows_all, 128), F32),
            pltpu.VMEM((rows_all, 128), F32),
            pltpu.VMEM((rows_all, 128), F32),
            pltpu.VMEM((rows_all, width), F32),
            pltpu.VMEM((2, 128, block), F32),
            pltpu.VMEM((2, block, 128), F32),
            pltpu.VMEM((steps, 144, block), F32),
            pltpu.VMEM((steps, 144, block), F32),
            pltpu.SemaphoreType.DMA((3,)),
            pltpu.SemaphoreType.DMA((6,)),
            pltpu.SemaphoreType.DMA((8,)),
            pltpu.SemaphoreType.DMA((4,)),
            pltpu.SemaphoreType.DMA((4,)),
            pltpu.SemaphoreType.DMA((6, n - 1)),
            pltpu.SemaphoreType.DMA((6, n - 1)),
            pltpu.SemaphoreType.DMA((8, nf)),
            pltpu.SemaphoreType.DMA((8, nf)),
            pltpu.SemaphoreType.DMA((steps,)),
            pltpu.SemaphoreType.DMA((steps,)),
        ],
        compiler_params=pltpu.CompilerParams(
            collective_id=0, has_side_effects=True, vmem_limit_bytes=60 * 2**20
        ),
        name="layer",
    )(
        earliest_past_snapshot,
        band_rows,
        score_scale,
        fields.reshape(lat_rows, local, width),
        lat_table,
        norm_gain.reshape(1, width),
        w_in1.reshape(2, block, block),
        b_in1,
        w_out2.reshape(2, block, block),
        b_out2,
        near,
        far,
        spec_cot.reshape(lat_rows, 2, modes, block).transpose(0, 1, 3, 2),
        w_query,
        w_keyval,
        w_output,
    )
    return (
        out.reshape(fields.shape),
        grads.reshape(2, 1, block, block),
        bias,
    )


def solution(mesh):
    placed = (
        P("dp", "frame", None, "lon", None),
        P("dp", None),
        P("dp"),
        P(),
        P(),
        P(None, "lon", None, None),
        P(None, "lon"),
        P(None, "lon", None, None),
        P(None, "lon"),
        P(),
        P(),
        P(),
        P(),
        P("dp", "frame", None, None, None, "lon"),
    )
    return jax.shard_map(
        body,
        mesh=mesh,
        in_specs=placed,
        out_specs=(P("dp", "frame", None, "lon", None), P(None, "lon", None, None), P(None, "lon")),
        check_vma=False,
    )
```

```python
import functools
import math

import jax
import jax.numpy as jnp
import numpy as np
from jax import lax
from jax.experimental import pallas as pl
from jax.experimental.pallas import tpu as pltpu
from jax.sharding import PartitionSpec as P

MESH = pl.DeviceIdType.MESH
EARLY = 3
F32 = jnp.float32
BF16 = jnp.bfloat16


def lanes_below(shape, bound):
    return lax.broadcasted_iota(jnp.int32, shape, len(shape) - 1) < bound


def split_two(value):
    high = value.astype(BF16)
    return high, (value - high.astype(F32)).astype(BF16)


def dot32(left, right, dims=(((1,), (0,)), ((), ()))):
    return lax.dot_general(left, right, dims, preferred_element_type=F32)


def angle_tables(length, local, parts, padded, modes, wide):
    near = np.zeros((2, padded, wide), np.float64)
    far = np.zeros((2, parts, 1, wide), np.float64)
    wave = np.arange(modes)
    turn = 2.0 * np.pi / length
    inner = (np.arange(local)[:, None] * wave[None, :]) % length
    near[0, :local, :modes] = np.cos(turn * inner)
    near[1, :local, :modes] = np.sin(turn * inner)
    outer = (np.arange(parts)[:, None] * local * wave[None, :]) % length
    far[0, :, 0, :modes] = np.cos(turn * outer)
    far[1, :, 0, :modes] = np.sin(turn * outer)
    return near.astype(np.float32), far.astype(np.float32)


def layer_kernel(
    geo,
    first_ref,
    band_ref,
    heads_ref,
    fields_ref,
    lat_ref,
    gain_ref,
    w1_ref,
    b1_ref,
    w2_ref,
    b2_ref,
    near_ref,
    far_ref,
    cot_ref,
    wq_hbm,
    wkv_hbm,
    wo_hbm,
    out_ref,
    grad_ref,
    bias_ref,
    embed,
    inputs_ref,
    wq,
    wkv,
    wo,
    table,
    mix1,
    mix2,
    brow,
    send1,
    recv1,
    send2,
    recv2,
    sendh_a,
    recvh_a,
    sendo_a,
    recvo_a,
    sendh_b,
    recvh_b,
    sendo_b,
    recvo_b,
    sendkv,
    recvkv,
    qs,
    kx,
    vx,
    scores,
    top,
    total,
    attended,
    acc,
    bias_acc,
    sums_send,
    sums_recv,
    weight_sem,
    own_z_sem,
    own_f_sem,
    kv_send,
    kv_recv,
    z_send,
    z_recv,
    f_send,
    f_recv,
    s_send,
    s_recv,
):
    n, nf, nd = geo["lon"], geo["frame"], geo["dp"]
    local, padded, modes, wide = geo["local"], geo["padded"], geo["modes"], geo["wide"]
    width, pieces = geo["width"], geo["pieces"]
    heads, kv_heads, hd = geo["heads"], geo["kv_heads"], geo["hd"]
    kv_width = kv_heads * hd
    sendh, recvh = (sendh_a, sendh_b), (recvh_a, recvh_b)
    sendo, recvo = (sendo_a, sendo_b), (recvo_a, recvo_b)
    scale_t = 1.0 / math.sqrt(local * n)
    me = lax.axis_index("lon")
    my_frame = lax.axis_index("frame")
    my_dp = lax.axis_index("dp")
    nx = nf // 2
    my_x, side = my_frame // 2, lax.rem(my_frame, 2)
    other_side = my_x * 2 + 1 - side

    def partner(index, bit):
        return index + bit * (1 - 2 * ((index // bit) % 2))

    sum_steps = []
    bit = 1
    while bit < nd:
        sum_steps.append(("dp", partner(my_dp, bit)))
        bit *= 2
    bit = 1
    while bit < nf:
        sum_steps.append(("frame", partner(my_frame, bit)))
        bit *= 2
    dp_partners = [who for axis, who in sum_steps if axis == "dp"]

    barrier = pltpu.get_barrier_semaphore()

    @pl.loop(1, n)
    def _(o):
        pl.semaphore_signal(
            barrier, inc=1, device_id={"lon": lax.rem(me + o, n)}, device_id_type=MESH
        )

    @pl.loop(1, nx)
    def _(o):
        pl.semaphore_signal(
            barrier,
            inc=1,
            device_id={"frame": lax.rem(my_x + o, nx) * 2 + side},
            device_id_type=MESH,
        )

    pl.semaphore_signal(barrier, inc=1, device_id={"frame": other_side}, device_id_type=MESH)

    for who in dp_partners:
        pl.semaphore_signal(barrier, inc=1, device_id={"dp": who}, device_id_type=MESH)

    weight_copies = [
        pltpu.make_async_copy(src, dst, weight_sem.at[i])
        for i, (src, dst) in enumerate(((wq_hbm, wq), (wkv_hbm, wkv), (wo_hbm, wo)))
    ]
    for copy in weight_copies:
        copy.start()

    rows_in = lat_ref.shape[0]
    picked = jnp.full((8, rows_in), band_ref[0, 0], jnp.int32)
    sublane = lax.broadcasted_iota(jnp.int32, (8, rows_in), 0)
    for r in range(1, band_ref.shape[1]):
        picked = jnp.where(sublane == r, band_ref[0, r], picked)
    onehot = (lax.broadcasted_iota(jnp.int32, (8, rows_in), 1) == picked).astype(BF16)
    looked_up = dot32(onehot, lat_ref[...])
    for r in range(band_ref.shape[1]):
        embed[r] = looked_up[r : r + 1]

    tail = local // 16 * 16
    send1[:, :, tail:, :] = jnp.zeros((2, n, padded - tail, 128), BF16)
    for piece, (start, span) in enumerate(pieces):
        slab = 2 * span // nx
        for k in range(nx // 2):
            if local - start - k * slab < slab:
                used = max(0, (local - start - k * slab) // 8 * 8)
                for r in range(2):
                    sendh[piece][:, r * nx // 2 + k, used:, :] = jnp.zeros(
                        (2, slab - used, width), BF16
                    )

    peers = n - 1

    def z_offset(i):
        return n // 2 + (i % 2) * ((i + 1) // 2) - (1 - i % 2) * (i // 2)

    def z_copy(src, dst, group, p, rows, i, target, slot):
        return pltpu.make_async_remote_copy(
            src_ref=src.at[p, target, rows],
            dst_ref=dst.at[p, slot, rows],
            send_sem=z_send.at[group, i],
            recv_sem=z_recv.at[group, i],
            device_id={"lon": target},
            device_id_type=MESH,
        )

    def z_own(src, dst, group, p, rows):
        return pltpu.make_async_copy(
            src.at[p, me, rows], dst.at[p, me, rows], own_z_sem.at[group]
        )

    def z_start(src, dst, group, p, rows):
        @pl.loop(0, peers)
        def _(i):
            target = lax.rem(me + z_offset(i), n)
            z_copy(src, dst, group, p, rows, i, target, me).start()

        z_own(src, dst, group, p, rows).start()

    def z_wait(src, dst, group, p, rows):
        z_own(src, dst, group, p, rows).wait()

        @pl.loop(0, peers)
        def _(i):
            peer = lax.rem(me + n - z_offset(i), n)
            z_copy(src, dst, group, p, rows, i, peer, peer).wait_recv()

    def z_sent(src, dst, group, p, rows):
        @pl.loop(0, peers)
        def _(i):
            target = lax.rem(me + z_offset(i), n)
            z_copy(src, dst, group, p, rows, i, target, me).wait_send()

    whole = pl.ds(0, padded)
    chunks = [(p, piece) for p in range(2) for piece in range(len(pieces))]

    def back_args(c):
        p, piece = chunks[c]
        return send2, recv2, 2 + c, p, pl.ds(*pieces[piece])

    def f_copy(src, dst, group, p, o, target, slot):
        return pltpu.make_async_remote_copy(
            src_ref=src.at[p, target],
            dst_ref=dst.at[p, slot],
            send_sem=f_send.at[group, o],
            recv_sem=f_recv.at[group, o],
            device_id={"frame": target * 2 + side},
            device_id_type=MESH,
        )

    def f_own(src, dst, group, p):
        return pltpu.make_async_copy(src.at[p, my_x], dst.at[p, my_x], own_f_sem.at[group])

    def f_start(src, dst, group, p):
        @pl.loop(1, nx)
        def _(o):
            f_copy(src, dst, group, p, o, lax.rem(my_x + o, nx), my_x).start()

        f_own(src, dst, group, p).start()

    def f_wait(src, dst, group, p):
        f_own(src, dst, group, p).wait()

        @pl.loop(1, nx)
        def _(o):
            peer = lax.rem(my_x + nx - o, nx)
            f_copy(src, dst, group, p, o, peer, peer).wait_recv()

    def f_sent(src, dst, group, p):
        @pl.loop(1, nx)
        def _(o):
            f_copy(src, dst, group, p, o, lax.rem(my_x + o, nx), my_x).wait_send()

    def kv_copy(c):
        rows = pl.ds(0, 2 * pieces[chunks[c][1]][1])
        return pltpu.make_async_remote_copy(
            src_ref=sendkv.at[c, rows],
            dst_ref=recvkv.at[c, rows],
            send_sem=kv_send.at[c],
            recv_sem=kv_recv.at[c],
            device_id={"frame": other_side},
            device_id_type=MESH,
        )

    def out_args(c):
        p, piece = chunks[c]
        return sendh[piece], recvh[piece], 2 * c, p

    def home_args(c):
        p, piece = chunks[c]
        return sendo[piece], recvo[piece], 2 * c + 1, p

    half = lanes_below((local, 128), 64)

    def normalize(p, r):
        cells = fields_ref[:, 2 * p + r, :].astype(F32) + embed[2 * p + r]
        inputs_ref[2 * p + r] = cells
        cells = cells - jnp.mean(cells, axis=-1, keepdims=True)
        spread = jnp.mean(cells * cells, axis=-1, keepdims=True)
        return cells * lax.rsqrt(spread + 1e-05) * gain_ref[...]

    def fill(p):
        row_a = normalize(p, 0)
        row_b = normalize(p, 1)
        for s in range(n // 2):
            part_a = row_a[:, s * 128 : (s + 1) * 128]
            part_b = row_b[:, s * 128 : (s + 1) * 128]
            even = jnp.where(half, part_a, pltpu.roll(part_b, 64, 1))
            odd = jnp.where(half, pltpu.roll(part_a, 64, 1), part_b)
            send1[p, 2 * s, 0:local, :] = even.astype(BF16)
            send1[p, 2 * s + 1, 0:local, :] = odd.astype(BF16)

    fill(0)
    pl.semaphore_wait(barrier, (n - 1) + nx + len(dp_partners))
    z_start(send1, recv1, 0, 0, whole)
    fill(1)
    z_start(send1, recv1, 1, 1, whole)

    near_cos, near_sin = near_ref[0], near_ref[1]

    @pl.loop(0, n)
    def _(s):
        far_cos, far_sin = far_ref[0, s], far_ref[1, s]
        rows = pl.ds(pl.multiple_of(s * padded, padded), padded)
        table[rows, 0:wide] = (near_cos * far_cos - near_sin * far_sin).astype(BF16)
        table[rows, wide : 2 * wide] = (-(near_sin * far_cos + near_cos * far_sin)).astype(BF16)

    columns = []
    for w_ref, mix, b_ref in ((w1_ref, mix1, b1_ref), (w2_ref, mix2, b2_ref)):
        brow[0:64, 0:64] = w_ref[0].astype(F32)
        brow[0:64, 64:128] = w_ref[1].astype(F32)
        brow[64:128, 0:64] = -w_ref[1].astype(F32)
        brow[64:128, 64:128] = w_ref[0].astype(F32)
        mix[...] = brow[...].T.astype(BF16)
        brow[0:1, 0:64] = b_ref[0:1, :]
        brow[0:1, 64:128] = b_ref[1:2, :]
        columns.append(jnp.broadcast_to(brow[0:1, :], (128, 128)).T[:, 0:1])
    column1, column2 = columns
    wave = lax.broadcasted_iota(jnp.int32, (128, wide), 1)
    factor = jnp.where(wave == 0, 1.0, 2.0)

    turned = (((1,), (1,)), ((), ()))
    acc[...] = jnp.zeros_like(acc)
    bias_acc[...] = jnp.zeros_like(bias_acc)

    def transform(p):
        z_wait(send1, recv1, p, p, whole)
        gathered = recv1[p].reshape(n * padded, 128)
        spectrum = dot32(gathered.T, table[...]) * scale_t
        cos_part = spectrum[:, 0:wide].astype(BF16)
        sin_part = spectrum[:, wide : 2 * wide].astype(BF16)
        mixed_re, mixed_im = [], []
        for r in range(2):
            stacked = jnp.concatenate(
                [cos_part[64 * r : 64 * r + 64], sin_part[64 * r : 64 * r + 64]], axis=0
            )
            first = jnp.maximum(dot32(mix1[...], stacked) + column1, 0.0).astype(BF16)
            second = (dot32(mix2[...], first) + column2).astype(BF16)
            second = (second.astype(F32) * factor).astype(BF16)
            mixed_re.append(second[0:64])
            mixed_im.append(second[64:128])
            for part in range(2):
                cot = cot_ref[2 * p + r, part]
                acc[part, 0:128, :] += dot32(first[:, 0:modes], cot, turned)
                bias_acc[part] += jnp.broadcast_to(
                    jnp.sum(cot.astype(F32), axis=1, keepdims=True), (64, 128)
                )
        grid = dot32(table[:, 0:wide], jnp.concatenate(mixed_re, axis=0), turned)
        grid = grid + dot32(table[:, wide : 2 * wide], jnp.concatenate(mixed_im, axis=0), turned)
        send2[p] = (grid * scale_t).astype(BF16).reshape(n, padded, 128)
        for c in range(len(chunks)):
            if chunks[c][0] == p:
                z_start(*back_args(c))

    transform(0)
    transform(1)

    sums_send[0, 0:64, :] = acc[0, 0:64, :] + acc[1, 64:128, :]
    sums_send[0, 64:128, :] = acc[1, 0:64, :] - acc[0, 64:128, :]
    for part in range(2):
        sums_send[0, 128 + 8 * part : 136 + 8 * part, :] = bias_acc[part].T[0:8, :]

    def sum_copy(i):
        axis, who = sum_steps[i]
        return pltpu.make_async_remote_copy(
            src_ref=sums_send.at[i],
            dst_ref=sums_recv.at[i],
            send_sem=s_send.at[i],
            recv_sem=s_recv.at[i],
            device_id={axis: who},
            device_id_type=MESH,
        )

    def finish_sum(i):
        sum_copy(i).wait()
        joined = sums_send[i] + sums_recv[i]
        if i + 1 < len(sum_steps):
            sums_send[i + 1] = joined
            sum_copy(i + 1).start()
        else:
            grad_ref[...] = joined[0:128]
            bias_ref[0:1, :] = joined[128:129]
            bias_ref[1:2, :] = joined[136:137]

    sum_copy(0).start()
    steps = len(sum_steps)
    early = min(EARLY, steps)
    for i in range(early):
        finish_sum(i)

    for copy in weight_copies:
        copy.wait()

    lane_head = lax.broadcasted_iota(jnp.int32, (width, 128), 0) // hd
    pool = (lane_head == lax.broadcasted_iota(jnp.int32, (width, 128), 1)).astype(BF16)
    head_lane = lax.broadcasted_iota(jnp.int32, (128, width), 1) // hd
    spread_heads = (head_lane == lax.broadcasted_iota(jnp.int32, (128, width), 0)).astype(BF16)
    head_ids = lax.broadcasted_iota(jnp.int32, (1, 128), 1)
    score_row = jnp.zeros((1, 128), F32)
    for h in range(heads):
        score_row = jnp.where(head_ids == h, heads_ref[h] * (1.0 / math.sqrt(hd)), score_row)
    groups = heads // kv_heads

    def head_norm(value, lanes):
        high, low = split_two(value * value)
        pooled = pool[0:lanes]
        mean = (dot32(high, pooled) + dot32(low, pooled)) * (1.0 / hd)
        high, low = split_two(lax.rsqrt(mean + 1e-06))
        wide_heads = spread_heads[:, 0:lanes]
        return value * (dot32(high, wide_heads) + dot32(low, wide_heads))

    def duplicate(value, ref, slot, half_id):
        rows_all = value.shape[0]
        half_all = lanes_below((rows_all, 128), 64)
        for j in range(kv_width // 128):
            part = value[:, j * 128 : (j + 1) * 128]
            rolled = pltpu.roll(part, 64, 1)
            low, high = slice(2 * j * 128, (2 * j + 1) * 128), slice(
                (2 * j + 1) * 128, (2 * j + 2) * 128
            )
            ref[slot, half_id, 0:rows_all, low] = jnp.where(half_all, part, rolled)
            ref[slot, half_id, 0:rows_all, high] = jnp.where(half_all, rolled, part)

    def per_query_head(ref, slot, half_id, t, slab):
        rows = slice(t * slab, (t + 1) * slab)
        parts = []
        for kh in range(kv_heads):
            parts += [ref[slot, half_id, rows, kh * 128 : (kh + 1) * 128]] * (groups // 2)
        return jnp.concatenate(parts, axis=1)

    def exchange(c):
        p, piece = chunks[c]
        start, span = pieces[piece]
        slab = 2 * span // nx
        z_wait(*back_args(c))
        count = min(span, local - start)
        near_half = lanes_below((count, 128), 64)
        for s in range(n // 2):
            lanes = slice(s * 128, (s + 1) * 128)
            even = recv2[p, 2 * s, start : start + count, :].astype(F32)
            odd = recv2[p, 2 * s + 1, start : start + count, :].astype(F32)
            grid_rows = (
                jnp.where(near_half, even, pltpu.roll(odd, 64, 1)),
                jnp.where(near_half, pltpu.roll(even, 64, 1), odd),
            )
            for r in range(2):
                inputs = inputs_ref[2 * p + r, start : start + count, lanes]
                hidden = (inputs + grid_rows[r]).astype(BF16)
                for k in range(nx // 2):
                    used = min(slab, count - k * slab)
                    if used > 0:
                        sendh[piece][p, r * nx // 2 + k, 0:used, lanes] = hidden[
                            k * slab : k * slab + used
                        ]
        f_start(*out_args(c))

    first_seen = first_ref[0]

    def project(c):
        p, piece = chunks[c]
        rows_all = 2 * pieces[piece][1]
        every = slice(0, rows_all)
        slot = c % 2
        f_wait(*out_args(c))
        tokens = recvh[piece][p].reshape(rows_all, width)
        keyval = dot32(tokens, wkv[...])
        keys = head_norm(keyval[:, 0:kv_width], kv_width).astype(BF16)
        values = keyval[:, kv_width:].astype(BF16)
        sendkv[c, every, 0:kv_width] = keys
        sendkv[c, every, kv_width : 2 * kv_width] = values
        kv_copy(c).start()
        query = head_norm(dot32(tokens, wq[...]), width)
        qs[slot, every, :] = query.astype(BF16).astype(F32)
        duplicate(keys.astype(F32), kx, slot, 0)
        duplicate(values.astype(F32), vx, slot, 0)

    def score_half(c, half_id):
        slab = 2 * pieces[chunks[c][1]][1] // nx
        slot = c % 2
        for j in range(nx):
            rows = slice(j * slab, nx * slab)
            count = nx - j
            product = (
                qs[slot, rows, :].reshape(count, slab, width)
                * per_query_head(kx, slot, half_id, j, slab)[None]
            ).reshape(count * slab, width)
            high, low = split_two(product)
            score = (dot32(high, pool) + dot32(low, pool)) * score_row
            frame = 2 * j + (side if half_id == 0 else 1 - side)
            seen = frame >= first_seen
            same = score[0:slab]
            if half_id == 1:
                same = jnp.where(jnp.logical_and(seen, side == 1), same, -1e30)
            if count > 1:
                later = jnp.where(seen, score[slab:], -1e30)
                score = jnp.concatenate([same, later], axis=0)
            else:
                score = same
            scores[half_id * nx + j, rows, :] = score
            top[rows, :] = jnp.maximum(top[rows, :], score)

    def attend(c):
        p, piece = chunks[c]
        rows_all = 2 * pieces[piece][1]
        slab = rows_all // nx
        every = slice(0, rows_all)
        slot = c % 2
        top[every, :] = jnp.full((rows_all, 128), -3e38, F32)
        score_half(c, 0)
        kv_copy(c).wait_recv()
        keyval = recvkv[c, every, :].astype(F32)
        duplicate(keyval[:, 0:kv_width], kx, slot, 1)
        duplicate(keyval[:, kv_width:], vx, slot, 1)
        score_half(c, 1)
        total[every, :] = jnp.zeros((rows_all, 128), F32)
        for t in range(2 * nx):
            rows = slice(t % nx * slab, rows_all)
            weight = jnp.exp(scores[t, rows, :] - top[rows, :])
            scores[t, rows, :] = weight
            total[rows, :] += weight
        attended[every, :] = jnp.zeros((rows_all, width), F32)
        for t in range(2 * nx):
            j = t % nx
            rows = slice(j * slab, rows_all)
            count = nx - j
            probs = (scores[t, rows, :] / total[rows, :]).astype(BF16)
            spread_probs = dot32(probs, spread_heads)
            attended[rows, :] += (
                spread_probs.reshape(count, slab, width)
                * per_query_head(vx, slot, t // nx, j, slab)[None]
            ).reshape(count * slab, width)
        tokens = recvh[piece][p].reshape(rows_all, width)
        output = dot32(attended[every, :].astype(BF16), wo[...])
        sendo[piece][p] = (tokens.astype(F32) + output).astype(BF16).reshape(nx, slab, width)
        f_start(*home_args(c))

    pending = list(range(early, steps))

    def next_sum():
        if pending:
            finish_sum(pending.pop(0))

    def deliver(c):
        p, piece = chunks[c]
        start, span = pieces[piece]
        slab = 2 * span // nx
        f_wait(*home_args(c))
        for r in range(2):
            for k in range(nx // 2):
                first = start + k * slab
                used = min(slab, local - first)
                if used > 0:
                    out_ref[2 * p + r, first : first + used, :] = recvo[piece][
                        p, r * nx // 2 + k, 0:used, :
                    ]

    last = len(chunks)
    exchange(0)
    next_sum()
    project(0)
    exchange(1)
    next_sum()
    project(1)
    attend(0)
    exchange(2)
    attend(1)
    project(2)
    exchange(3)
    deliver(0)
    deliver(1)
    project(3)
    attend(2)
    attend(3)
    while pending:
        next_sum()

    deliver(2)
    deliver(3)

    for p in range(2):
        z_sent(send1, recv1, p, p, whole)
    for c in range(last):
        z_sent(*back_args(c))
        f_sent(*out_args(c))
        f_sent(*home_args(c))
        kv_copy(c).wait_send()


def keep(grads_ref, bias_ref, grads_out, bias_out):
    grads_out[...] = grads_ref[...]
    bias_out[...] = bias_ref[...]


def body(
    fields,
    band_rows,
    earliest_past_snapshot,
    lat_table,
    norm_gain,
    w_in1,
    b_in1,
    w_out2,
    b_out2,
    w_query,
    w_keyval,
    w_output,
    score_scale,
    spec_cot,
):
    _, _, lat_rows, local, width = fields.shape
    n = lax.axis_size("lon")
    nf = lax.axis_size("frame")
    nd = lax.axis_size("dp")
    modes = spec_cot.shape[4]
    block = w_in1.shape[2]
    heads = score_scale.shape[0]
    hd = width // heads
    kv_heads = w_keyval.shape[1] // 2 // hd
    padded = -(-local // 16) * 16
    wide = -(-modes // 128) * 128
    nx = nf // 2
    units = 2 * padded // nx // 16
    split = (units + 1) // 2 * 8 * nx
    pieces = ((0, split), (split, padded - split))
    rows_all = 2 * split
    geo = dict(
        lon=n,
        frame=nf,
        dp=nd,
        local=local,
        padded=padded,
        modes=modes,
        wide=wide,
        width=width,
        pieces=pieces,
        heads=heads,
        kv_heads=kv_heads,
        hd=hd,
    )
    near, far = angle_tables(local * n, local, n, padded, modes, wide)
    steps = int(math.log2(nd)) + int(math.log2(nf))
    vmem = pl.BlockSpec(memory_space=pltpu.VMEM)
    smem = pl.BlockSpec(memory_space=pltpu.SMEM)
    anywhere = pl.BlockSpec(memory_space=pl.ANY)
    out, grads, bias = pl.pallas_call(
        functools.partial(layer_kernel, geo),
        out_shape=(
            jax.ShapeDtypeStruct((lat_rows, local, width), BF16),
            jax.ShapeDtypeStruct((2 * block, block), F32),
            jax.ShapeDtypeStruct((2, block), F32),
        ),
        in_specs=[smem] * 3 + [vmem] * 10 + [anywhere] * 3,
        out_specs=(vmem, vmem, vmem),
        scratch_shapes=[
            pltpu.VMEM((lat_rows, 1, width), F32),
            pltpu.VMEM((lat_rows, local, width), F32),
            pltpu.VMEM(w_query.shape, BF16),
            pltpu.VMEM(w_keyval.shape, BF16),
            pltpu.VMEM(w_output.shape, BF16),
            pltpu.VMEM((n * padded, 2 * wide), BF16),
            pltpu.VMEM((128, 128), BF16),
            pltpu.VMEM((128, 128), BF16),
            pltpu.VMEM((128, 128), F32),
        ]
        + [pltpu.VMEM((2, n, padded, 128), BF16)] * 4
        + [pltpu.VMEM((2, nx, 2 * pieces[0][1] // nx, width), BF16)] * 4
        + [pltpu.VMEM((2, nx, 2 * pieces[1][1] // nx, width), BF16)] * 4
        + [
            pltpu.VMEM((4, rows_all, w_keyval.shape[1]), BF16),
            pltpu.VMEM((4, rows_all, w_keyval.shape[1]), BF16),
            pltpu.VMEM((2, rows_all, width), F32),
            pltpu.VMEM((2, 2, rows_all, kv_heads * 128), F32),
            pltpu.VMEM((2, 2, rows_all, kv_heads * 128), F32),
            pltpu.VMEM((nf, rows_all, 128), F32),
            pltpu.VMEM((rows_all, 128), F32),
            pltpu.VMEM((rows_all, 128), F32),
            pltpu.VMEM((rows_all, width), F32),
            pltpu.VMEM((2, 128, block), F32),
            pltpu.VMEM((2, block, 128), F32),
            pltpu.VMEM((steps, 144, block), F32),
            pltpu.VMEM((steps, 144, block), F32),
            pltpu.SemaphoreType.DMA((3,)),
            pltpu.SemaphoreType.DMA((6,)),
            pltpu.SemaphoreType.DMA((8,)),
            pltpu.SemaphoreType.DMA((4,)),
            pltpu.SemaphoreType.DMA((4,)),
            pltpu.SemaphoreType.DMA((6, n - 1)),
            pltpu.SemaphoreType.DMA((6, n - 1)),
            pltpu.SemaphoreType.DMA((8, nf)),
            pltpu.SemaphoreType.DMA((8, nf)),
            pltpu.SemaphoreType.DMA((steps,)),
            pltpu.SemaphoreType.DMA((steps,)),
        ],
        compiler_params=pltpu.CompilerParams(
            collective_id=0, has_side_effects=True, vmem_limit_bytes=60 * 2**20
        ),
        name="layer",
    )(
        earliest_past_snapshot,
        band_rows,
        score_scale,
        fields.reshape(lat_rows, local, width).transpose(1, 0, 2),
        lat_table,
        norm_gain.reshape(1, width),
        w_in1.reshape(2, block, block),
        b_in1,
        w_out2.reshape(2, block, block),
        b_out2,
        near,
        far,
        spec_cot.reshape(lat_rows, 2, modes, block).transpose(0, 1, 3, 2),
        w_query,
        w_keyval,
        w_output,
    )
    grads, bias = pl.pallas_call(
        keep,
        out_shape=(
            jax.ShapeDtypeStruct(grads.shape, F32),
            jax.ShapeDtypeStruct(bias.shape, F32),
        ),
        in_specs=[vmem] * 2,
        out_specs=(vmem, vmem),
        name="sums",
    )(grads, bias)
    return (
        out.reshape(fields.shape),
        grads.reshape(2, 1, block, block),
        bias,
    )


def solution(mesh):
    placed = (
        P("dp", "frame", None, "lon", None),
        P("dp", None),
        P("dp"),
        P(),
        P(),
        P(None, "lon", None, None),
        P(None, "lon"),
        P(None, "lon", None, None),
        P(None, "lon"),
        P(),
        P(),
        P(),
        P(),
        P("dp", "frame", None, None, None, "lon"),
    )
    return jax.shard_map(
        body,
        mesh=mesh,
        in_specs=placed,
        out_specs=(P("dp", "frame", None, "lon", None), P(None, "lon", None, None), P(None, "lon")),
        check_vma=False,
    )
```

```python
import functools
import math

import jax
import jax.numpy as jnp
import numpy as np
from jax import lax
from jax.experimental import pallas as pl
from jax.experimental.pallas import tpu as pltpu
from jax.sharding import PartitionSpec as P

MESH = pl.DeviceIdType.MESH
EARLY = 3
F32 = jnp.float32
BF16 = jnp.bfloat16


def lanes_below(shape, bound):
    return lax.broadcasted_iota(jnp.int32, shape, len(shape) - 1) < bound


def split_two(value):
    high = value.astype(BF16)
    return high, (value - high.astype(F32)).astype(BF16)


def dot32(left, right, dims=(((1,), (0,)), ((), ()))):
    return lax.dot_general(left, right, dims, preferred_element_type=F32)


def angle_tables(length, local, parts, padded, modes, wide):
    near = np.zeros((2, padded, wide), np.float64)
    far = np.zeros((2, parts, 1, wide), np.float64)
    wave = np.arange(modes)
    turn = 2.0 * np.pi / length
    inner = (np.arange(local)[:, None] * wave[None, :]) % length
    near[0, :local, :modes] = np.cos(turn * inner)
    near[1, :local, :modes] = np.sin(turn * inner)
    outer = (np.arange(parts)[:, None] * local * wave[None, :]) % length
    far[0, :, 0, :modes] = np.cos(turn * outer)
    far[1, :, 0, :modes] = np.sin(turn * outer)
    return near.astype(np.float32), far.astype(np.float32)


def layer_kernel(
    geo,
    first_ref,
    band_ref,
    heads_ref,
    fields_ref,
    lat_ref,
    gain_ref,
    w1_ref,
    b1_ref,
    w2_ref,
    b2_ref,
    near_ref,
    far_ref,
    cot_ref,
    wq_hbm,
    wkv_hbm,
    wo_hbm,
    out_ref,
    grad_ref,
    bias_ref,
    embed,
    inputs_ref,
    wq,
    wkv,
    wo,
    table,
    mix1,
    mix2,
    brow,
    send1,
    recv1,
    send2,
    recv2,
    sendh_a,
    recvh_a,
    sendo_a,
    recvo_a,
    sendh_b,
    recvh_b,
    sendo_b,
    recvo_b,
    sendkv,
    recvkv,
    qs,
    kx,
    vx,
    scores,
    top,
    total,
    attended,
    acc,
    bias_acc,
    sums_send,
    sums_recv,
    weight_sem,
    own_z_sem,
    own_f_sem,
    kv_send,
    kv_recv,
    z_send,
    z_recv,
    f_send,
    f_recv,
    s_send,
    s_recv,
):
    n, nf, nd = geo["lon"], geo["frame"], geo["dp"]
    local, padded, modes, wide = geo["local"], geo["padded"], geo["modes"], geo["wide"]
    width, pieces = geo["width"], geo["pieces"]
    heads, kv_heads, hd = geo["heads"], geo["kv_heads"], geo["hd"]
    kv_width = kv_heads * hd
    sendh, recvh = (sendh_a, sendh_b), (recvh_a, recvh_b)
    sendo, recvo = (sendo_a, sendo_b), (recvo_a, recvo_b)
    scale_t = 1.0 / math.sqrt(local * n)
    me = lax.axis_index("lon")
    my_frame = lax.axis_index("frame")
    my_dp = lax.axis_index("dp")
    nx = nf // 2
    my_x, side = my_frame // 2, lax.rem(my_frame, 2)
    other_side = my_x * 2 + 1 - side

    def partner(index, bit):
        return index + bit * (1 - 2 * ((index // bit) % 2))

    sum_steps = []
    bit = 1
    while bit < nd:
        sum_steps.append(("dp", partner(my_dp, bit)))
        bit *= 2
    bit = 1
    while bit < nf:
        sum_steps.append(("frame", partner(my_frame, bit)))
        bit *= 2
    dp_partners = [who for axis, who in sum_steps if axis == "dp"]

    barrier = pltpu.get_barrier_semaphore()

    @pl.loop(1, n)
    def _(o):
        pl.semaphore_signal(
            barrier, inc=1, device_id={"lon": lax.rem(me + o, n)}, device_id_type=MESH
        )

    @pl.loop(1, nx)
    def _(o):
        pl.semaphore_signal(
            barrier,
            inc=1,
            device_id={"frame": lax.rem(my_x + o, nx) * 2 + side},
            device_id_type=MESH,
        )

    pl.semaphore_signal(barrier, inc=1, device_id={"frame": other_side}, device_id_type=MESH)

    for who in dp_partners:
        pl.semaphore_signal(barrier, inc=1, device_id={"dp": who}, device_id_type=MESH)

    weight_copies = [
        pltpu.make_async_copy(src, dst, weight_sem.at[i])
        for i, (src, dst) in enumerate(((wq_hbm, wq), (wkv_hbm, wkv), (wo_hbm, wo)))
    ]
    for copy in weight_copies:
        copy.start()

    rows_in = lat_ref.shape[0]
    picked = jnp.full((8, rows_in), band_ref[0, 0], jnp.int32)
    sublane = lax.broadcasted_iota(jnp.int32, (8, rows_in), 0)
    for r in range(1, band_ref.shape[1]):
        picked = jnp.where(sublane == r, band_ref[0, r], picked)
    onehot = (lax.broadcasted_iota(jnp.int32, (8, rows_in), 1) == picked).astype(BF16)
    looked_up = dot32(onehot, lat_ref[...])
    for r in range(band_ref.shape[1]):
        embed[r] = looked_up[r : r + 1]

    tail = local // 16 * 16
    send1[:, :, tail:, :] = jnp.zeros((2, n, padded - tail, 128), BF16)
    for piece, (start, span) in enumerate(pieces):
        slab = 2 * span // nx
        for k in range(nx // 2):
            if local - start - k * slab < slab:
                used = max(0, (local - start - k * slab) // 8 * 8)
                for r in range(2):
                    sendh[piece][:, r * nx // 2 + k, used:, :] = jnp.zeros(
                        (2, slab - used, width), BF16
                    )

    peers = n - 1

    def z_offset(i):
        return n // 2 + (i % 2) * ((i + 1) // 2) - (1 - i % 2) * (i // 2)

    def z_copy(src, dst, group, p, rows, i, target, slot):
        return pltpu.make_async_remote_copy(
            src_ref=src.at[p, target, rows],
            dst_ref=dst.at[p, slot, rows],
            send_sem=z_send.at[group, i],
            recv_sem=z_recv.at[group, i],
            device_id={"lon": target},
            device_id_type=MESH,
        )

    def z_own(src, dst, group, p, rows):
        return pltpu.make_async_copy(
            src.at[p, me, rows], dst.at[p, me, rows], own_z_sem.at[group]
        )

    def z_start(src, dst, group, p, rows):
        @pl.loop(0, peers)
        def _(i):
            target = lax.rem(me + z_offset(i), n)
            z_copy(src, dst, group, p, rows, i, target, me).start()

        z_own(src, dst, group, p, rows).start()

    def z_wait(src, dst, group, p, rows):
        z_own(src, dst, group, p, rows).wait()

        @pl.loop(0, peers)
        def _(i):
            peer = lax.rem(me + n - z_offset(i), n)
            z_copy(src, dst, group, p, rows, i, peer, peer).wait_recv()

    def z_sent(src, dst, group, p, rows):
        @pl.loop(0, peers)
        def _(i):
            target = lax.rem(me + z_offset(i), n)
            z_copy(src, dst, group, p, rows, i, target, me).wait_send()

    whole = pl.ds(0, padded)
    chunks = [(p, piece) for p in range(2) for piece in range(len(pieces))]

    def back_args(c):
        p, piece = chunks[c]
        return send2, recv2, 2 + c, p, pl.ds(*pieces[piece])

    def f_copy(src, dst, group, p, o, target, slot):
        return pltpu.make_async_remote_copy(
            src_ref=src.at[p, target],
            dst_ref=dst.at[p, slot],
            send_sem=f_send.at[group, o],
            recv_sem=f_recv.at[group, o],
            device_id={"frame": target * 2 + side},
            device_id_type=MESH,
        )

    def f_own(src, dst, group, p):
        return pltpu.make_async_copy(src.at[p, my_x], dst.at[p, my_x], own_f_sem.at[group])

    def f_start(src, dst, group, p):
        @pl.loop(1, nx)
        def _(o):
            f_copy(src, dst, group, p, o, lax.rem(my_x + o, nx), my_x).start()

        f_own(src, dst, group, p).start()

    def f_wait(src, dst, group, p):
        f_own(src, dst, group, p).wait()

        @pl.loop(1, nx)
        def _(o):
            peer = lax.rem(my_x + nx - o, nx)
            f_copy(src, dst, group, p, o, peer, peer).wait_recv()

    def f_sent(src, dst, group, p):
        @pl.loop(1, nx)
        def _(o):
            f_copy(src, dst, group, p, o, lax.rem(my_x + o, nx), my_x).wait_send()

    def kv_copy(c):
        rows = pl.ds(0, 2 * pieces[chunks[c][1]][1])
        return pltpu.make_async_remote_copy(
            src_ref=sendkv.at[c, rows],
            dst_ref=recvkv.at[c, rows],
            send_sem=kv_send.at[c],
            recv_sem=kv_recv.at[c],
            device_id={"frame": other_side},
            device_id_type=MESH,
        )

    def out_args(c):
        p, piece = chunks[c]
        return sendh[piece], recvh[piece], 2 * c, p

    def home_args(c):
        p, piece = chunks[c]
        return sendo[piece], recvo[piece], 2 * c + 1, p

    half = lanes_below((local, 128), 64)

    def normalize(p, r):
        cells = fields_ref[:, 2 * p + r, :].astype(F32) + embed[2 * p + r]
        inputs_ref[2 * p + r] = cells
        cells = cells - jnp.mean(cells, axis=-1, keepdims=True)
        spread = jnp.mean(cells * cells, axis=-1, keepdims=True)
        return cells * lax.rsqrt(spread + 1e-05) * gain_ref[...]

    def fill(p):
        row_a = normalize(p, 0)
        row_b = normalize(p, 1)
        for s in range(n // 2):
            part_a = row_a[:, s * 128 : (s + 1) * 128]
            part_b = row_b[:, s * 128 : (s + 1) * 128]
            even = jnp.where(half, part_a, pltpu.roll(part_b, 64, 1))
            odd = jnp.where(half, pltpu.roll(part_a, 64, 1), part_b)
            send1[p, 2 * s, 0:local, :] = even.astype(BF16)
            send1[p, 2 * s + 1, 0:local, :] = odd.astype(BF16)

    fill(0)
    pl.semaphore_wait(barrier, (n - 1) + nx + len(dp_partners))
    z_start(send1, recv1, 0, 0, whole)
    fill(1)
    z_start(send1, recv1, 1, 1, whole)

    near_cos, near_sin = near_ref[0], near_ref[1]

    @pl.loop(0, n)
    def _(s):
        far_cos, far_sin = far_ref[0, s], far_ref[1, s]
        rows = pl.ds(pl.multiple_of(s * padded, padded), padded)
        table[rows, 0:wide] = (near_cos * far_cos - near_sin * far_sin).astype(BF16)
        table[rows, wide : 2 * wide] = (-(near_sin * far_cos + near_cos * far_sin)).astype(BF16)

    columns = []
    for w_ref, mix, b_ref in ((w1_ref, mix1, b1_ref), (w2_ref, mix2, b2_ref)):
        brow[0:64, 0:64] = w_ref[0].astype(F32)
        brow[0:64, 64:128] = w_ref[1].astype(F32)
        brow[64:128, 0:64] = -w_ref[1].astype(F32)
        brow[64:128, 64:128] = w_ref[0].astype(F32)
        mix[...] = brow[...].T.astype(BF16)
        brow[0:1, 0:64] = b_ref[0:1, :]
        brow[0:1, 64:128] = b_ref[1:2, :]
        columns.append(jnp.broadcast_to(brow[0:1, :], (128, 128)).T[:, 0:1])
    column1, column2 = columns
    wave = lax.broadcasted_iota(jnp.int32, (128, wide), 1)
    factor = jnp.where(wave == 0, 1.0, 2.0)

    turned = (((1,), (1,)), ((), ()))
    acc[...] = jnp.zeros_like(acc)
    bias_acc[...] = jnp.zeros_like(bias_acc)

    def transform(p):
        z_wait(send1, recv1, p, p, whole)
        gathered = recv1[p].reshape(n * padded, 128)
        spectrum = dot32(gathered.T, table[...]) * scale_t
        cos_part = spectrum[:, 0:wide].astype(BF16)
        sin_part = spectrum[:, wide : 2 * wide].astype(BF16)
        mixed_re, mixed_im = [], []
        for r in range(2):
            stacked = jnp.concatenate(
                [cos_part[64 * r : 64 * r + 64], sin_part[64 * r : 64 * r + 64]], axis=0
            )
            first = jnp.maximum(dot32(mix1[...], stacked) + column1, 0.0).astype(BF16)
            second = (dot32(mix2[...], first) + column2).astype(BF16)
            second = (second.astype(F32) * factor).astype(BF16)
            mixed_re.append(second[0:64])
            mixed_im.append(second[64:128])
            for part in range(2):
                cot = cot_ref[2 * p + r, part]
                acc[part, 0:128, :] += dot32(first[:, 0:modes], cot, turned)
                bias_acc[part] += jnp.broadcast_to(
                    jnp.sum(cot.astype(F32), axis=1, keepdims=True), (64, 128)
                )
        grid = dot32(table[:, 0:wide], jnp.concatenate(mixed_re, axis=0), turned)
        grid = grid + dot32(table[:, wide : 2 * wide], jnp.concatenate(mixed_im, axis=0), turned)
        send2[p] = (grid * scale_t).astype(BF16).reshape(n, padded, 128)
        for c in range(len(chunks)):
            if chunks[c][0] == p:
                z_start(*back_args(c))

    transform(0)
    transform(1)

    sums_send[0, 0:64, :] = acc[0, 0:64, :] + acc[1, 64:128, :]
    sums_send[0, 64:128, :] = acc[1, 0:64, :] - acc[0, 64:128, :]
    for part in range(2):
        sums_send[0, 128 + 8 * part : 136 + 8 * part, :] = bias_acc[part].T[0:8, :]

    def sum_copy(i):
        axis, who = sum_steps[i]
        return pltpu.make_async_remote_copy(
            src_ref=sums_send.at[i],
            dst_ref=sums_recv.at[i],
            send_sem=s_send.at[i],
            recv_sem=s_recv.at[i],
            device_id={axis: who},
            device_id_type=MESH,
        )

    def finish_sum(i):
        sum_copy(i).wait()
        joined = sums_send[i] + sums_recv[i]
        if i + 1 < len(sum_steps):
            sums_send[i + 1] = joined
            sum_copy(i + 1).start()
        else:
            grad_ref[...] = joined[0:128]
            bias_ref[0:1, :] = joined[128:129]
            bias_ref[1:2, :] = joined[136:137]

    sum_copy(0).start()
    steps = len(sum_steps)
    early = min(EARLY, steps)
    for i in range(early):
        finish_sum(i)

    for copy in weight_copies:
        copy.wait()

    lane_head = lax.broadcasted_iota(jnp.int32, (width, 128), 0) // hd
    pool = (lane_head == lax.broadcasted_iota(jnp.int32, (width, 128), 1)).astype(BF16)
    head_lane = lax.broadcasted_iota(jnp.int32, (128, width), 1) // hd
    spread_heads = (head_lane == lax.broadcasted_iota(jnp.int32, (128, width), 0)).astype(BF16)
    head_ids = lax.broadcasted_iota(jnp.int32, (1, 128), 1)
    score_row = jnp.zeros((1, 128), F32)
    for h in range(heads):
        score_row = jnp.where(head_ids == h, heads_ref[h] * (1.0 / math.sqrt(hd)), score_row)
    groups = heads // kv_heads

    def head_norm(value, lanes):
        high, low = split_two(value * value)
        pooled = pool[0:lanes]
        mean = (dot32(high, pooled) + dot32(low, pooled)) * (1.0 / hd)
        high, low = split_two(lax.rsqrt(mean + 1e-06))
        wide_heads = spread_heads[:, 0:lanes]
        return value * (dot32(high, wide_heads) + dot32(low, wide_heads))

    def duplicate(value, ref, slot, half_id):
        rows_all = value.shape[0]
        half_all = lanes_below((rows_all, 128), 64)
        for j in range(kv_width // 128):
            part = value[:, j * 128 : (j + 1) * 128]
            rolled = pltpu.roll(part, 64, 1)
            low, high = slice(2 * j * 128, (2 * j + 1) * 128), slice(
                (2 * j + 1) * 128, (2 * j + 2) * 128
            )
            ref[slot, half_id, 0:rows_all, low] = jnp.where(half_all, part, rolled)
            ref[slot, half_id, 0:rows_all, high] = jnp.where(half_all, rolled, part)

    def per_query_head(ref, slot, half_id, t, slab):
        rows = slice(t * slab, (t + 1) * slab)
        parts = []
        for kh in range(kv_heads):
            parts += [ref[slot, half_id, rows, kh * 128 : (kh + 1) * 128]] * (groups // 2)
        return jnp.concatenate(parts, axis=1)

    def exchange(c):
        p, piece = chunks[c]
        start, span = pieces[piece]
        slab = 2 * span // nx
        z_wait(*back_args(c))
        count = min(span, local - start)
        near_half = lanes_below((count, 128), 64)
        for s in range(n // 2):
            lanes = slice(s * 128, (s + 1) * 128)
            even = recv2[p, 2 * s, start : start + count, :].astype(F32)
            odd = recv2[p, 2 * s + 1, start : start + count, :].astype(F32)
            grid_rows = (
                jnp.where(near_half, even, pltpu.roll(odd, 64, 1)),
                jnp.where(near_half, pltpu.roll(even, 64, 1), odd),
            )
            for r in range(2):
                inputs = inputs_ref[2 * p + r, start : start + count, lanes]
                hidden = (inputs + grid_rows[r]).astype(BF16)
                for k in range(nx // 2):
                    used = min(slab, count - k * slab)
                    if used > 0:
                        sendh[piece][p, r * nx // 2 + k, 0:used, lanes] = hidden[
                            k * slab : k * slab + used
                        ]
        f_start(*out_args(c))

    first_seen = first_ref[0]

    def project(c):
        p, piece = chunks[c]
        rows_all = 2 * pieces[piece][1]
        every = slice(0, rows_all)
        slot = c % 2
        f_wait(*out_args(c))
        tokens = recvh[piece][p].reshape(rows_all, width)
        keyval = dot32(tokens, wkv[...])
        keys = head_norm(keyval[:, 0:kv_width], kv_width).astype(BF16)
        values = keyval[:, kv_width:].astype(BF16)
        sendkv[c, every, 0:kv_width] = keys
        sendkv[c, every, kv_width : 2 * kv_width] = values
        kv_copy(c).start()
        query = head_norm(dot32(tokens, wq[...]), width)
        qs[slot, every, :] = query.astype(BF16).astype(F32)
        duplicate(keys.astype(F32), kx, slot, 0)
        duplicate(values.astype(F32), vx, slot, 0)

    def score_half(c, half_id):
        slab = 2 * pieces[chunks[c][1]][1] // nx
        slot = c % 2
        for j in range(nx):
            rows = slice(j * slab, nx * slab)
            count = nx - j
            product = (
                qs[slot, rows, :].reshape(count, slab, width)
                * per_query_head(kx, slot, half_id, j, slab)[None]
            ).reshape(count * slab, width)
            high, low = split_two(product)
            score = (dot32(high, pool) + dot32(low, pool)) * score_row
            frame = 2 * j + (side if half_id == 0 else 1 - side)
            seen = frame >= first_seen
            same = score[0:slab]
            if half_id == 1:
                same = jnp.where(jnp.logical_and(seen, side == 1), same, -1e30)
            if count > 1:
                later = jnp.where(seen, score[slab:], -1e30)
                score = jnp.concatenate([same, later], axis=0)
            else:
                score = same
            scores[half_id * nx + j, rows, :] = score
            top[rows, :] = jnp.maximum(top[rows, :], score)

    def attend(c):
        p, piece = chunks[c]
        rows_all = 2 * pieces[piece][1]
        slab = rows_all // nx
        every = slice(0, rows_all)
        slot = c % 2
        top[every, :] = jnp.full((rows_all, 128), -3e38, F32)
        score_half(c, 0)
        kv_copy(c).wait_recv()
        keyval = recvkv[c, every, :].astype(F32)
        duplicate(keyval[:, 0:kv_width], kx, slot, 1)
        duplicate(keyval[:, kv_width:], vx, slot, 1)
        score_half(c, 1)
        total[every, :] = jnp.zeros((rows_all, 128), F32)
        for t in range(2 * nx):
            rows = slice(t % nx * slab, rows_all)
            weight = jnp.exp(scores[t, rows, :] - top[rows, :])
            scores[t, rows, :] = weight
            total[rows, :] += weight
        attended[every, :] = jnp.zeros((rows_all, width), F32)
        for t in range(2 * nx):
            j = t % nx
            rows = slice(j * slab, rows_all)
            count = nx - j
            probs = (scores[t, rows, :] / total[rows, :]).astype(BF16)
            spread_probs = dot32(probs, spread_heads)
            attended[rows, :] += (
                spread_probs.reshape(count, slab, width)
                * per_query_head(vx, slot, t // nx, j, slab)[None]
            ).reshape(count * slab, width)
        tokens = recvh[piece][p].reshape(rows_all, width)
        output = dot32(attended[every, :].astype(BF16), wo[...])
        sendo[piece][p] = (tokens.astype(F32) + output).astype(BF16).reshape(nx, slab, width)
        f_start(*home_args(c))

    pending = list(range(early, steps))

    def next_sum():
        if pending:
            finish_sum(pending.pop(0))

    def deliver(c):
        p, piece = chunks[c]
        start, span = pieces[piece]
        slab = 2 * span // nx
        f_wait(*home_args(c))
        for r in range(2):
            for k in range(nx // 2):
                first = start + k * slab
                used = min(slab, local - first)
                if used > 0:
                    out_ref[first : first + used, 2 * p + r, :] = recvo[piece][
                        p, r * nx // 2 + k, 0:used, :
                    ]

    last = len(chunks)
    exchange(0)
    next_sum()
    project(0)
    exchange(1)
    next_sum()
    project(1)
    attend(0)
    exchange(2)
    attend(1)
    project(2)
    exchange(3)
    deliver(0)
    deliver(1)
    project(3)
    attend(2)
    attend(3)
    while pending:
        next_sum()

    deliver(2)
    deliver(3)

    for p in range(2):
        z_sent(send1, recv1, p, p, whole)
    for c in range(last):
        z_sent(*back_args(c))
        f_sent(*out_args(c))
        f_sent(*home_args(c))
        kv_copy(c).wait_send()


def keep(grads_ref, bias_ref, grads_out, bias_out):
    grads_out[...] = grads_ref[...]
    bias_out[...] = bias_ref[...]


def body(
    fields,
    band_rows,
    earliest_past_snapshot,
    lat_table,
    norm_gain,
    w_in1,
    b_in1,
    w_out2,
    b_out2,
    w_query,
    w_keyval,
    w_output,
    score_scale,
    spec_cot,
):
    _, _, lat_rows, local, width = fields.shape
    n = lax.axis_size("lon")
    nf = lax.axis_size("frame")
    nd = lax.axis_size("dp")
    modes = spec_cot.shape[4]
    block = w_in1.shape[2]
    heads = score_scale.shape[0]
    hd = width // heads
    kv_heads = w_keyval.shape[1] // 2 // hd
    padded = -(-local // 16) * 16
    wide = -(-modes // 128) * 128
    nx = nf // 2
    units = 2 * padded // nx // 16
    split = (units + 1) // 2 * 8 * nx
    pieces = ((0, split), (split, padded - split))
    rows_all = 2 * split
    geo = dict(
        lon=n,
        frame=nf,
        dp=nd,
        local=local,
        padded=padded,
        modes=modes,
        wide=wide,
        width=width,
        pieces=pieces,
        heads=heads,
        kv_heads=kv_heads,
        hd=hd,
    )
    near, far = angle_tables(local * n, local, n, padded, modes, wide)
    steps = int(math.log2(nd)) + int(math.log2(nf))
    vmem = pl.BlockSpec(memory_space=pltpu.VMEM)
    smem = pl.BlockSpec(memory_space=pltpu.SMEM)
    anywhere = pl.BlockSpec(memory_space=pl.ANY)
    out, grads, bias = pl.pallas_call(
        functools.partial(layer_kernel, geo),
        out_shape=(
            jax.ShapeDtypeStruct((local, lat_rows, width), BF16),
            jax.ShapeDtypeStruct((2 * block, block), F32),
            jax.ShapeDtypeStruct((2, block), F32),
        ),
        in_specs=[smem] * 3 + [vmem] * 10 + [anywhere] * 3,
        out_specs=(vmem, vmem, vmem),
        scratch_shapes=[
            pltpu.VMEM((lat_rows, 1, width), F32),
            pltpu.VMEM((lat_rows, local, width), F32),
            pltpu.VMEM(w_query.shape, BF16),
            pltpu.VMEM(w_keyval.shape, BF16),
            pltpu.VMEM(w_output.shape, BF16),
            pltpu.VMEM((n * padded, 2 * wide), BF16),
            pltpu.VMEM((128, 128), BF16),
            pltpu.VMEM((128, 128), BF16),
            pltpu.VMEM((128, 128), F32),
        ]
        + [pltpu.VMEM((2, n, padded, 128), BF16)] * 4
        + [pltpu.VMEM((2, nx, 2 * pieces[0][1] // nx, width), BF16)] * 4
        + [pltpu.VMEM((2, nx, 2 * pieces[1][1] // nx, width), BF16)] * 4
        + [
            pltpu.VMEM((4, rows_all, w_keyval.shape[1]), BF16),
            pltpu.VMEM((4, rows_all, w_keyval.shape[1]), BF16),
            pltpu.VMEM((2, rows_all, width), F32),
            pltpu.VMEM((2, 2, rows_all, kv_heads * 128), F32),
            pltpu.VMEM((2, 2, rows_all, kv_heads * 128), F32),
            pltpu.VMEM((nf, rows_all, 128), F32),
            pltpu.VMEM((rows_all, 128), F32),
            pltpu.VMEM((rows_all, 128), F32),
            pltpu.VMEM((rows_all, width), F32),
            pltpu.VMEM((2, 128, block), F32),
            pltpu.VMEM((2, block, 128), F32),
            pltpu.VMEM((steps, 144, block), F32),
            pltpu.VMEM((steps, 144, block), F32),
            pltpu.SemaphoreType.DMA((3,)),
            pltpu.SemaphoreType.DMA((6,)),
            pltpu.SemaphoreType.DMA((8,)),
            pltpu.SemaphoreType.DMA((4,)),
            pltpu.SemaphoreType.DMA((4,)),
            pltpu.SemaphoreType.DMA((6, n - 1)),
            pltpu.SemaphoreType.DMA((6, n - 1)),
            pltpu.SemaphoreType.DMA((8, nf)),
            pltpu.SemaphoreType.DMA((8, nf)),
            pltpu.SemaphoreType.DMA((steps,)),
            pltpu.SemaphoreType.DMA((steps,)),
        ],
        compiler_params=pltpu.CompilerParams(
            collective_id=0, has_side_effects=True, vmem_limit_bytes=60 * 2**20
        ),
        name="layer",
    )(
        earliest_past_snapshot,
        band_rows,
        score_scale,
        fields.reshape(lat_rows, local, width).transpose(1, 0, 2),
        lat_table,
        norm_gain.reshape(1, width),
        w_in1.reshape(2, block, block),
        b_in1,
        w_out2.reshape(2, block, block),
        b_out2,
        near,
        far,
        spec_cot.reshape(lat_rows, 2, modes, block).transpose(0, 1, 3, 2),
        w_query,
        w_keyval,
        w_output,
    )
    grads, bias = pl.pallas_call(
        keep,
        out_shape=(
            jax.ShapeDtypeStruct(grads.shape, F32),
            jax.ShapeDtypeStruct(bias.shape, F32),
        ),
        in_specs=[vmem] * 2,
        out_specs=(vmem, vmem),
        name="sums",
    )(grads, bias)
    return (
        out.transpose(1, 0, 2).reshape(fields.shape),
        grads.reshape(2, 1, block, block),
        bias,
    )


def solution(mesh):
    placed = (
        P("dp", "frame", None, "lon", None),
        P("dp", None),
        P("dp"),
        P(),
        P(),
        P(None, "lon", None, None),
        P(None, "lon"),
        P(None, "lon", None, None),
        P(None, "lon"),
        P(),
        P(),
        P(),
        P(),
        P("dp", "frame", None, None, None, "lon"),
    )
    return jax.shard_map(
        body,
        mesh=mesh,
        in_specs=placed,
        out_specs=(P("dp", "frame", None, "lon", None), P(None, "lon", None, None), P(None, "lon")),
        check_vma=False,
    )
```
